512 devices in a mesh: seq: 32 (over z_lo, y), blk: 8 (over x, core), grp: 2 (over z_hi).
Axes of the slice: x: 4, y: 8, z: 8 (z_hi: 2, z_lo: 4; z = z_hi * 4 + z_lo), core: 2. Of those that a mesh axis runs over, the one named last changes fastest.
Arguments:
- activations: bfloat16 [32768, 8192], P('seq', 'blk'), may hold values from -23 to 23
- cotangent: bfloat16 [32768, 1024], P('seq'), may hold values from -0.0625 to 0.0625
- factor: float32 [8192, 1024], P('blk', ('seq', 'grp')), may hold values from -0.3 to 1.7
Outputs:
- new_factor: float32 [8192, 1024], P('blk', ('seq', 'grp'))
- direction: float32 [8192, 1024], P('blk', ('seq', 'grp'))
The draws below stay inside these ranges and needn't reach their ends.
All inputs are finite; a program needn't handle non-finite values.
Results may differ from the reference program's by a relative error of at most 0.007.
Values may be sent and summed in bfloat16 or wider, within the bound.
No kernel may reach another device: no remote copies, remote signals or barrier semaphores. Data moves between devices by JAX's collectives and lax.ppermute only.
A program may use at most 64 MiB of HBM per device.

```python
import math
import jax
import jax.numpy as jnp

B = 1024
DOUT = 1024
D = 8192
TOKENS = 32768


def draw_activations(key, part):
    first, second, third = jax.random.split(key, 3)
    values = jnp.clip(jax.random.normal(first, (TOKENS, D), jnp.float32), -4.0, 4.0)
    row_scale = jnp.exp(jax.random.uniform(second, (TOKENS, 1), jnp.float32, math.log(0.2), math.log(2.0)))
    rising = jnp.sqrt(0.5 + 1.5 * jnp.arange(TOKENS, dtype=jnp.float32) / TOKENS)[:, None]
    column_scale = jnp.exp(jax.random.uniform(third, (1, D), jnp.float32, math.log(0.5), math.log(2.0)))
    return (values * row_scale * rising * column_scale).astype(jnp.bfloat16)


def draw_factor(key, part):
    first, second = jax.random.split(key, 2)
    spread = 0.5 / math.sqrt(B)
    off_diag = jnp.clip(jax.random.normal(first, (D, B), jnp.float32), -4.0, 4.0) * spread
    diag_scale = jnp.exp(jax.random.uniform(second, (D, 1), jnp.float32, math.log(0.7), math.log(1.4)))
    on_diag = (jnp.arange(D)[:, None] % B == jnp.arange(B)[None, :]).astype(jnp.float32)
    return off_diag + on_diag * diag_scale


def with_spikes(result, rng, source, target, blocks, factor):
    def block_of(axis_at):
        return (jnp.arange(result.shape[axis_at]) // (result.shape[axis_at] // blocks)).reshape((-1,) + (1,) * (result.ndim - 1 - axis_at))

    first = jax.random.permutation(rng, blocks)[block_of(target)]
    far = (block_of(target) + blocks // 2) % blocks
    return jnp.where((block_of(source) == first) | (block_of(source) == far), factor * result, result)


def steps_of(stream_key, dims, cuts, least, largest):
    factor_of, own = 1.0, jax.random.fold_in(stream_key, 6)
    for axis_at, blocks in cuts:
        heights = jnp.exp(jax.random.uniform(jax.random.fold_in(own, axis_at), (blocks,), jnp.float32, least / len(cuts), largest / len(cuts)))
        factor_of = factor_of * jnp.repeat(heights, dims[axis_at] // blocks).reshape([-1 if axis == axis_at else 1 for axis in range(len(dims))])
    return factor_of


def noise_with(rng, dims, width, limit, cuts, heavy, held_as=jnp.bfloat16):
    array = width * jax.random.normal(rng, dims, jnp.float32)
    if cuts:
        array = array * steps_of(rng, dims, cuts, -0.22, 0.18)
    return jnp.clip(with_spikes(array, jax.random.fold_in(rng, 3), *heavy), -limit, limit).astype(held_as)


def setup_inputs(seed: int = 0) -> dict:
    key_list = jax.random.split(jax.random.key(seed), 4)
    activations = draw_activations(jax.random.fold_in(key_list[3], 71), 0)
    cotangent = noise_with(key_list[1], (TOKENS, DOUT), (TOKENS ** -0.5), 0.0625, ((0, 32),), (0, 1, 32, 2.75))
    factor = draw_factor(jax.random.fold_in(key_list[3], 71), 0)
    return {"activations": activations, "cotangent": cotangent, "factor": factor}


damping = 0.25
step_size = 0.4


def reference(activations, cotangent, factor):
    factor_low = factor.astype(jnp.bfloat16)
    identity = jnp.eye(B, dtype=jnp.float32)
    new_blocks = []
    direction_blocks = []
    for block in range(D // B):
        block_factor = factor_low[block * B:(block + 1) * B]
        inputs = activations[:, block * B:(block + 1) * B]
        whitened = jnp.dot(inputs, block_factor, preferred_element_type=jnp.float32).astype(jnp.bfloat16)
        gram = jnp.dot(whitened.T, whitened, preferred_element_type=jnp.float32)
        cross = jnp.dot(block_factor.T, block_factor, preferred_element_type=jnp.float32)
        curvature = (gram / TOKENS + damping * cross - identity).astype(jnp.bfloat16)
        update = jnp.dot(block_factor, curvature, preferred_element_type=jnp.float32)
        new_blocks.append(factor[block * B:(block + 1) * B] - 0.5 * step_size * update)
        gradient = jnp.dot(inputs.T, cotangent, preferred_element_type=jnp.float32).astype(jnp.bfloat16)
        half = jnp.dot(block_factor.T, gradient, preferred_element_type=jnp.float32).astype(jnp.bfloat16)
        direction_blocks.append(jnp.dot(block_factor, half, preferred_element_type=jnp.float32))
    return jnp.concatenate(new_blocks, axis=0), jnp.concatenate(direction_blocks, axis=0)
```

```python
import jax
import jax.numpy as jnp
from jax import lax
from jax.sharding import Mesh
from jax.sharding import PartitionSpec as P

SEQ = ("seq_0", "seq_1")
SEQ_GRP = ("seq_0", "seq_1", "grp")


damping = 0.25
step_size = 0.4


def class_groups(seq_count):
    return [[q * 2 + (h ^ (q & 1)) for q in range(seq_count)] for h in range(2)]


def exchange(blocks, groups):
    return lax.all_to_all(
        blocks, SEQ_GRP, split_axis=0, concat_axis=0, tiled=True, axis_index_groups=groups
    )


def class_rows(matrix, seq_count, owned, chosen):
    shaped = matrix.reshape(seq_count // 2, 2, 2, owned, matrix.shape[1])
    even = lax.dynamic_index_in_dim(shaped[:, 0], chosen, 1)
    odd = lax.dynamic_index_in_dim(shaped[:, 1], 1 - chosen, 1)
    return jnp.concatenate([even, odd], axis=1).reshape(seq_count, owned, matrix.shape[1])


def on_device(activations, cotangent, factor):
    f32, bf16 = jnp.float32, jnp.bfloat16
    seq_count = lax.axis_size(SEQ)
    y_count = lax.axis_size("seq_1")
    seq_index = lax.axis_index(SEQ)
    chosen = lax.axis_index("grp") ^ (seq_index & 1)
    owned = factor.shape[1]
    width = factor.shape[0]
    half_width = width // 2
    total_tokens = activations.shape[0] * seq_count
    groups = class_groups(seq_count)
    tokens_first = (((0,), (0,)), ((), ()))
    rows_rows = (((1,), (1,)), ((), ()))

    own = factor.T
    own_low = own.astype(bf16)
    near = exchange(jnp.broadcast_to(own_low[None], (seq_count, owned, width)), groups)
    near = near.reshape(half_width, width)

    gradient_part = lax.dot_general(
        cotangent, activations, tokens_first, preferred_element_type=f32
    ).astype(bf16)
    gradient_blocks = exchange(class_rows(gradient_part, seq_count, owned, chosen), groups)

    far = lax.ppermute(near, "seq_1", [(y, y ^ 1) for y in range(y_count)])

    whitened = lax.dot_general(near, activations, rows_rows, preferred_element_type=f32).astype(bf16)
    moment = jnp.dot(whitened, activations, preferred_element_type=f32).astype(bf16)
    moment_blocks = exchange(moment.reshape(seq_count, owned, width), groups)

    gradient = gradient_blocks.astype(f32).sum(axis=0).astype(bf16)
    half_near = lax.dot_general(gradient, near, rows_rows, preferred_element_type=f32).astype(bf16)
    half_far = lax.dot_general(gradient, far, rows_rows, preferred_element_type=f32).astype(bf16)
    direction = jnp.dot(half_near, near, preferred_element_type=f32) + jnp.dot(
        half_far, far, preferred_element_type=f32
    )

    inner = (
        moment_blocks.astype(f32).sum(axis=0) / total_tokens + damping * own_low.astype(f32)
    ).astype(bf16)
    identity = (
        jnp.arange(half_width, dtype=jnp.int32)[None, :]
        == (seq_index * owned + jnp.arange(owned, dtype=jnp.int32))[:, None]
    ).astype(f32)
    curve_near = (
        lax.dot_general(inner, near, rows_rows, preferred_element_type=f32) - identity
    ).astype(bf16)
    curve_far = lax.dot_general(inner, far, rows_rows, preferred_element_type=f32).astype(bf16)
    update = jnp.dot(curve_near, near, preferred_element_type=f32) + jnp.dot(
        curve_far, far, preferred_element_type=f32
    )
    new_factor = own - 0.5 * step_size * update
    return (new_factor.T, direction.T)


def solution(mesh):
    torus = Mesh(
        mesh.devices.reshape(4, 8, mesh.shape["blk"], mesh.shape["grp"]),
        ("seq_0", "seq_1", "blk", "grp"),
    )
    return jax.shard_map(
        on_device,
        mesh=torus,
        in_specs=(P(SEQ, "blk"), P(SEQ, None), P("blk", SEQ_GRP)),
        out_specs=(P("blk", SEQ_GRP), P("blk", SEQ_GRP)),
        check_vma=False,
    )
```

```python
import functools

import jax
import jax.numpy as jnp
from jax import lax
from jax.experimental import pallas as pl
from jax.experimental.pallas import tpu as pltpu
from jax.sharding import Mesh
from jax.sharding import PartitionSpec as P

SEQ = ("seq_0", "seq_1")
SEQ_GRP = ("seq_0", "seq_1", "grp")


damping = 0.25
step_size = 0.4

f32, bf16 = jnp.float32, jnp.bfloat16
VMEM_LIMIT = 16 * 1024 * 1024
ROWS_ROWS = (((1,), (1,)), ((), ()))
TOKENS_FIRST = (((0,), (0,)), ((), ()))


def member(z_low, y, grp):
    return (z_low * 8 + y) * 2 + grp


def of_class(h, yh, zh, a, b):
    return member(2 * zh + b, 2 * yh + a, h ^ (yh & 1))


SQUARES = [
    [of_class(h, yh, zh, a, b) for a in range(2) for b in range(2)]
    for h in range(2)
    for yh in range(4)
    for zh in range(2)
]
FAR_GROUPS = [
    [of_class(h, yh, zh, a, b) for yh in range(4) for zh in range(2)]
    for h in range(2)
    for a in range(2)
    for b in range(2)
]
ACROSS = [(y, (y + 1) % 8 if y % 2 else (y - 1) % 8) for y in range(8)]
ALL_MEMBERS = [(z, y, g) for z in range(4) for y in range(8) for g in range(2)]
TURNED = {
    d: [(member(z, y, g), member(z ^ (d & 1), y ^ (d >> 1), g)) for z, y, g in ALL_MEMBERS]
    for d in (1, 2, 3)
}


def exchange(blocks, groups):
    return lax.all_to_all(
        blocks, SEQ_GRP, split_axis=0, concat_axis=0, tiled=True, axis_index_groups=groups
    )


def vmem():
    return pl.BlockSpec(memory_space=pltpu.VMEM)


def position():
    z_low, y, grp = lax.axis_index("seq_0"), lax.axis_index("seq_1"), lax.axis_index("grp")
    yh = y // 2
    return y % 2, z_low % 2, yh, z_low // 2, (grp + yh) % 2


def pick_kernel(rows_ref, *out_refs):
    a, b, _, _, h = position()
    for d, out_ref in enumerate(out_refs):
        a_there = 1 - a if d & 2 else a
        b_there = 1 - b if d & 1 else b
        for f in range(8):
            row, column = f >> 1, f & 1
            grp = 1 - h if row & 1 else h
            out_ref[f] = rows_ref[member(2 * column + b_there, 2 * row + a_there, grp)]


def pick(rows):
    shape = jax.ShapeDtypeStruct((8,) + rows.shape[1:], rows.dtype)
    return pl.pallas_call(
        pick_kernel,
        out_shape=[shape] * 4,
        in_specs=[vmem()],
        out_specs=[vmem()] * 4,
        compiler_params=pltpu.CompilerParams(vmem_limit_bytes=VMEM_LIMIT),
        name="pick",
    )(rows)


def join_kernel(moment_ref, own_ref, *refs):
    others, out_ref = refs[:3], refs[3]
    for f in range(8):
        total = moment_ref[0, f].astype(f32)
        for k in range(1, 4):
            total = total + moment_ref[k, f].astype(f32)
        out_ref[f, :16] = total.astype(bf16)
        total = own_ref[f].astype(f32)
        for other in others:
            total = total + other[f].astype(f32)
        out_ref[f, 16:] = total.astype(bf16)


def join(moment, own, others):
    return pl.pallas_call(
        join_kernel,
        out_shape=jax.ShapeDtypeStruct((8, 32, own.shape[2]), bf16),
        in_specs=[vmem()] * 5,
        out_specs=vmem(),
        compiler_params=pltpu.CompilerParams(vmem_limit_bytes=VMEM_LIMIT),
        name="join",
    )(moment, own, *others)


def finish_kernel(tokens, sums_ref, near_ref, far_ref, own_ref, new_ref, direction_ref):
    a, b, yh, zh, _ = position()
    at = ((2 * a + b) * 8 + 2 * yh + zh) * 16
    own = own_ref[...]
    total = sums_ref[0].astype(f32)
    for k in range(1, 8):
        total = total + sums_ref[k].astype(f32)
    inner = total[:16] / tokens + damping * own.astype(bf16).astype(f32)
    high = inner.astype(bf16)
    low = (inner - high.astype(f32)).astype(bf16)
    left = jnp.concatenate([high, low, total[16:].astype(bf16)], axis=0)
    result = jnp.zeros((32, own.shape[1]), f32)
    for k, ref in enumerate((near_ref, far_ref)):
        rows = ref[...]
        product = lax.dot_general(left, rows, ROWS_ROWS, preferred_element_type=f32)
        curve = product[:16] + product[16:32]
        if k == 0:
            column = lax.broadcasted_iota(jnp.int32, curve.shape, 1)
            row = lax.broadcasted_iota(jnp.int32, curve.shape, 0)
            curve = curve - (column == row + at).astype(f32)
        right = jnp.concatenate([curve.astype(bf16), product[32:].astype(bf16)], axis=0)
        result = result + jnp.dot(right, rows, preferred_element_type=f32)
    new_ref[...] = own - 0.5 * step_size * result[:16]
    direction_ref[...] = result[16:]


def finish(tokens, sums, near, far, own):
    return pl.pallas_call(
        functools.partial(finish_kernel, tokens),
        out_shape=[jax.ShapeDtypeStruct(own.shape, f32)] * 2,
        in_specs=[vmem()] * 4,
        out_specs=[vmem()] * 2,
        compiler_params=pltpu.CompilerParams(vmem_limit_bytes=VMEM_LIMIT),
        name="finish",
    )(sums, near, far, own)


def on_device(activations, cotangent, factor):
    seq_count = lax.axis_size(SEQ)
    owned = factor.shape[1]
    width = factor.shape[0]
    half_width = width // 2
    total_tokens = activations.shape[0] * seq_count

    own = factor.T
    own_low = own.astype(bf16)
    square = exchange(jnp.broadcast_to(own_low[None], (8, owned, width)), FAR_GROUPS)
    square = square.reshape(1, 8 * owned, width)
    near = exchange(jnp.broadcast_to(square, (4, 8 * owned, width)), SQUARES)
    near = near.reshape(half_width, width)

    gradient_part = lax.dot_general(
        cotangent, activations, TOKENS_FIRST, preferred_element_type=f32
    ).astype(bf16)
    parts = pick(gradient_part.reshape(2 * seq_count, owned, width))
    arrived = [lax.ppermute(parts[d], SEQ_GRP, TURNED[d]) for d in (1, 2, 3)]

    whitened = lax.dot_general(near, activations, ROWS_ROWS, preferred_element_type=f32).astype(bf16)
    moment = jnp.dot(whitened, activations, preferred_element_type=f32).astype(bf16)
    moment = exchange(moment.reshape(4, 8 * owned, width), SQUARES)
    far = lax.ppermute(near, "seq_1", ACROSS)
    sums = exchange(join(moment.reshape(4, 8, owned, width), parts[0], arrived), FAR_GROUPS)

    new_factor, direction = finish(total_tokens, sums, near, far, own)
    return (new_factor.T, direction.T)


def solution(mesh):
    torus = Mesh(
        mesh.devices.reshape(4, 8, mesh.shape["blk"], mesh.shape["grp"]),
        ("seq_0", "seq_1", "blk", "grp"),
    )
    return jax.shard_map(
        on_device,
        mesh=torus,
        in_specs=(P(SEQ, "blk"), P(SEQ, None), P("blk", SEQ_GRP)),
        out_specs=(P("blk", SEQ_GRP), P("blk", SEQ_GRP)),
        check_vma=False,
    )
```

```python
import functools

import jax
import jax.numpy as jnp
from jax import lax
from jax.experimental import pallas as pl
from jax.experimental.pallas import tpu as pltpu
from jax.sharding import Mesh
from jax.sharding import PartitionSpec as P

SEQ = ("seq_0", "seq_1")
SEQ_GRP = ("seq_0", "seq_1", "grp")


damping = 0.25
step_size = 0.4

f32, bf16 = jnp.float32, jnp.bfloat16
VMEM_LIMIT = 16 * 1024 * 1024
ROWS_ROWS = (((1,), (1,)), ((), ()))
TOKENS_FIRST = (((0,), (0,)), ((), ()))


def member(z_low, y, grp):
    return (z_low * 8 + y) * 2 + grp


def of_class(h, yh, zh, a, b):
    return member(2 * zh + b, 2 * yh + a, h ^ (yh & 1))


FAR_GROUPS = [
    [of_class(h, yh, zh, a, b) for yh in range(4) for zh in range(2)]
    for h in range(2)
    for a in range(2)
    for b in range(2)
]
ACROSS = [(y, (y + 1) % 8 if y % 2 else (y - 1) % 8) for y in range(8)]
ALL_MEMBERS = [(z, y, g) for z in range(4) for y in range(8) for g in range(2)]
TURNED = {
    d: [(member(z, y, g), member(z ^ (d & 1), y ^ (d >> 1), g)) for z, y, g in ALL_MEMBERS]
    for d in (1, 2, 3)
}


def exchange(blocks, groups):
    return lax.all_to_all(
        blocks, SEQ_GRP, split_axis=0, concat_axis=0, tiled=True, axis_index_groups=groups
    )


def vmem():
    return pl.BlockSpec(memory_space=pltpu.VMEM)


def position():
    z_low, y, grp = lax.axis_index("seq_0"), lax.axis_index("seq_1"), lax.axis_index("grp")
    yh = y // 2
    return y % 2, z_low % 2, yh, z_low // 2, (grp + yh) % 2


def pick_kernel(rows_ref, *out_refs):
    a, b, _, _, h = position()
    for d, out_ref in enumerate(out_refs):
        a_there = 1 - a if d & 2 else a
        b_there = 1 - b if d & 1 else b
        for f in range(8):
            row, column = f >> 1, f & 1
            grp = 1 - h if row & 1 else h
            out_ref[f] = rows_ref[member(2 * column + b_there, 2 * row + a_there, grp)]


def pick(rows):
    shape = jax.ShapeDtypeStruct((8,) + rows.shape[1:], rows.dtype)
    return pl.pallas_call(
        pick_kernel,
        out_shape=[shape] * 4,
        in_specs=[vmem()],
        out_specs=[vmem()] * 4,
        compiler_params=pltpu.CompilerParams(vmem_limit_bytes=VMEM_LIMIT),
        name="pick",
    )(rows)


def moment_kernel(rows_ref, x_ref, out_ref):
    x = x_ref[...]
    whitened = lax.dot_general(rows_ref[...], x, ROWS_ROWS, preferred_element_type=f32)
    out_ref[...] = jnp.dot(whitened.astype(bf16), x, preferred_element_type=f32).astype(bf16)


def moment_of(rows, x):
    return pl.pallas_call(
        moment_kernel,
        out_shape=jax.ShapeDtypeStruct(rows.shape, bf16),
        in_specs=[vmem()] * 2,
        out_specs=vmem(),
        compiler_params=pltpu.CompilerParams(vmem_limit_bytes=VMEM_LIMIT),
        cost_estimate=pl.CostEstimate(
            flops=4 * rows.size * x.shape[0], bytes_accessed=2 * x.size, transcendentals=0
        ),
        name="moment",
    )(rows, x)


def join_kernel(*refs):
    ins, out_ref = refs[:8], refs[8]
    for f in range(8):
        for first, parts in ((0, ins[:4]), (16, ins[4:])):
            total = parts[0][f].astype(f32)
            for part in parts[1:]:
                total = total + part[f].astype(f32)
            out_ref[f, first : first + 16] = total.astype(bf16)


def join(moments, gradients):
    width = gradients[0].shape[2]
    moments = [m.reshape(8, 16, width) for m in moments]
    return pl.pallas_call(
        join_kernel,
        out_shape=jax.ShapeDtypeStruct((8, 32, width), bf16),
        in_specs=[vmem()] * 8,
        out_specs=vmem(),
        compiler_params=pltpu.CompilerParams(vmem_limit_bytes=VMEM_LIMIT),
        name="join",
    )(*moments, *gradients)


def finish_kernel(tokens, sums_ref, near_ref, far_ref, own_ref, new_ref, direction_ref):
    _, _, yh, zh, _ = position()
    at = (2 * yh + zh) * 16
    own = own_ref[...]
    total = sums_ref[0].astype(f32)
    for k in range(1, 8):
        total = total + sums_ref[k].astype(f32)
    inner = total[:16] / tokens + damping * own.astype(bf16).astype(f32)
    high = inner.astype(bf16)
    low = (inner - high.astype(f32)).astype(bf16)
    left = jnp.concatenate([high, low, total[16:].astype(bf16)], axis=0)
    result = jnp.zeros((32, own.shape[1]), f32)
    for k, ref in enumerate((near_ref, far_ref)):
        rows = ref[...]
        product = lax.dot_general(left, rows, ROWS_ROWS, preferred_element_type=f32)
        curve = product[:16] + product[16:32]
        if k == 0:
            column = lax.broadcasted_iota(jnp.int32, curve.shape, 1)
            row = lax.broadcasted_iota(jnp.int32, curve.shape, 0)
            curve = curve - (column == row + at).astype(f32)
        right = jnp.concatenate([curve.astype(bf16), product[32:].astype(bf16)], axis=0)
        result = result + jnp.dot(right, rows, preferred_element_type=f32)
    new_ref[...] = own - 0.5 * step_size * result[:16]
    direction_ref[...] = result[16:]


def finish(tokens, sums, near, far, own):
    return pl.pallas_call(
        functools.partial(finish_kernel, tokens),
        out_shape=[jax.ShapeDtypeStruct(own.shape, f32)] * 2,
        in_specs=[vmem()] * 4,
        out_specs=[vmem()] * 2,
        compiler_params=pltpu.CompilerParams(vmem_limit_bytes=VMEM_LIMIT),
        name="finish",
    )(sums, near, far, own)


def on_device(activations, cotangent, factor):
    seq_count = lax.axis_size(SEQ)
    owned = factor.shape[1]
    width = factor.shape[0]
    total_tokens = activations.shape[0] * seq_count

    def turn(block, d):
        return lax.ppermute(block, SEQ_GRP, TURNED[d])

    own = factor.T
    own_low = own.astype(bf16)
    with jax.named_scope("k_far"):
        block = exchange(jnp.broadcast_to(own_low[None], (8, owned, width)), FAR_GROUPS)

    gradient_part = lax.dot_general(
        cotangent, activations, TOKENS_FIRST, preferred_element_type=f32
    ).astype(bf16)
    parts = pick(gradient_part.reshape(2 * seq_count, owned, width))
    block, *parts = lax.optimization_barrier((block, *parts))
    with jax.named_scope("g_near"):
        gradients = [parts[0]] + [turn(parts[d], d) for d in (1, 2, 3)]

    block = block.reshape(8 * owned, width)
    with jax.named_scope("k_near"):
        blocks = [block] + [turn(block, d) for d in (1, 2, 3)]
    moments = [moment_of(rows, activations) for rows in blocks]
    with jax.named_scope("p_near"):
        moments = [moments[0]] + [turn(moments[d], d) for d in (1, 2, 3)]
    near = jnp.concatenate(blocks, axis=0)
    with jax.named_scope("k_across"):
        far = lax.ppermute(near, "seq_1", ACROSS)
    with jax.named_scope("p_far"):
        sums = exchange(join(moments, gradients), FAR_GROUPS)

    new_factor, direction = finish(total_tokens, sums, near, far, own)
    return (new_factor.T, direction.T)


def solution(mesh):
    torus = Mesh(
        mesh.devices.reshape(4, 8, mesh.shape["blk"], mesh.shape["grp"]),
        ("seq_0", "seq_1", "blk", "grp"),
    )
    return jax.shard_map(
        on_device,
        mesh=torus,
        in_specs=(P(SEQ, "blk"), P(SEQ, None), P("blk", SEQ_GRP)),
        out_specs=(P("blk", SEQ_GRP), P("blk", SEQ_GRP)),
        check_vma=False,
    )
```

```python
import functools

import jax
import jax.numpy as jnp
from jax import lax
from jax.experimental import pallas as pl
from jax.experimental.pallas import tpu as pltpu
from jax.sharding import Mesh
from jax.sharding import PartitionSpec as P

SEQ = ("seq_0", "seq_1")
SEQ_GRP = ("seq_0", "seq_1", "grp")


damping = 0.25
step_size = 0.4

f32, bf16 = jnp.float32, jnp.bfloat16
VMEM_LIMIT = 16 * 1024 * 1024
ROWS_ROWS = (((1,), (1,)), ((), ()))
TOKENS_FIRST = (((0,), (0,)), ((), ()))


def member(z_low, y, grp):
    return (z_low * 8 + y) * 2 + grp


def of_class(h, yh, zh, a, b):
    return member(2 * zh + b, 2 * yh + a, h ^ (yh & 1))


FAR_GROUPS = [
    [of_class(h, yh, zh, a, b) for yh in range(4) for zh in range(2)]
    for h in range(2)
    for a in range(2)
    for b in range(2)
]
COSETS = [FAR_GROUPS[k] + FAR_GROUPS[k + 4] for k in range(4)]


def outer(at):
    return (at - 1) % 8 if at % 2 == 0 else (at + 1) % 8


def moves(step_z, step_y):
    pairs = []
    for z in range(8):
        for y in range(8):
            there_z, there_y = step_z(z), step_y(y)
            pairs.append((member(z % 4, y, z // 4), member(there_z % 4, there_y, there_z // 4)))
    return pairs


def stay(at):
    return at


def inner(at):
    return at ^ 1


INNER = {1: moves(inner, stay), 2: moves(stay, inner), 3: moves(inner, inner)}
OUTER = {1: moves(outer, stay), 2: moves(stay, outer), 3: moves(outer, outer)}


def exchange(blocks, groups):
    return lax.all_to_all(
        blocks, SEQ_GRP, split_axis=0, concat_axis=0, tiled=True, axis_index_groups=groups
    )


def vmem():
    return pl.BlockSpec(memory_space=pltpu.VMEM)


def hbm():
    return pl.BlockSpec(memory_space=pltpu.HBM)


def run_copies(pairs, sems):
    copies = [pltpu.make_async_copy(*pair, sems.at[k]) for k, pair in enumerate(pairs)]
    for copy in copies:
        copy.start()
    return copies


def position():
    z_low, y, grp = lax.axis_index("seq_0"), lax.axis_index("seq_1"), lax.axis_index("grp")
    yh = y // 2
    return y % 2, z_low % 2, yh, z_low // 2, (grp + yh) % 2


def call(kernel, out_shape, in_specs, out_specs, *args, **more):
    return pl.pallas_call(
        kernel,
        out_shape=out_shape,
        in_specs=in_specs,
        out_specs=out_specs,
        compiler_params=pltpu.CompilerParams(vmem_limit_bytes=VMEM_LIMIT),
        **more,
    )(*args)


def spread_kernel(own_ref, out_ref, low, sems):
    low[...] = own_ref[...].astype(bf16)
    for copy in run_copies([(low, out_ref.at[k]) for k in range(out_ref.shape[0])], sems):
        copy.wait()


def spread(own, count):
    shape = pltpu.HBM((count,) + own.shape, bf16)
    scratch = [pltpu.VMEM(own.shape, bf16), pltpu.SemaphoreType.DMA((count,))]
    return call(spread_kernel, shape, [vmem()], hbm(), own, scratch_shapes=scratch)


def mine_kernel(blocks_ref, out_ref):
    out_ref[...] = blocks_ref[position()[4]]


def own_class(blocks):
    shape = jax.ShapeDtypeStruct(blocks.shape[1:], bf16)
    return call(mine_kernel, shape, [vmem()], vmem(), blocks)


def others_kernel(blocks_ref, other_ref, side_ref, corner_ref, sems):
    _, b, yh, zh, h = position()
    z_low, grp = 2 * zh + b, (h + yh) % 2
    turn = jnp.where((z_low == 0) | (z_low == 3), 1, 0)
    side_class = (grp + turn + yh) % 2
    pairs = [
        (blocks_ref.at[1 - h], other_ref),
        (blocks_ref.at[1 - side_class], side_ref),
        (blocks_ref.at[side_class], corner_ref),
    ]
    for copy in run_copies(pairs, sems):
        copy.wait()


def others(blocks):
    shape = pltpu.HBM(blocks.shape[1:], bf16)
    scratch = [pltpu.SemaphoreType.DMA((3,))]
    return call(others_kernel, [shape] * 3, [vmem()], [hbm()] * 3, blocks, scratch_shapes=scratch)


def pick_kernel(rows_ref, *refs):
    out_refs, sems = refs[:4], refs[4]
    a, b, _, _, h = position()
    pairs = []
    for d, out_ref in enumerate(out_refs):
        a_there = 1 - a if d & 2 else a
        b_there = 1 - b if d & 1 else b
        for f in range(8):
            row, column = f >> 1, f & 1
            grp = 1 - h if row & 1 else h
            there = member(2 * column + b_there, 2 * row + a_there, grp)
            pairs.append((rows_ref.at[there], out_ref.at[f]))
    for copy in run_copies(pairs, sems):
        copy.wait()


def pick(rows):
    shape = pltpu.HBM((8,) + rows.shape[1:], rows.dtype)
    scratch = [pltpu.SemaphoreType.DMA((32,))]
    return call(pick_kernel, [shape] * 4, [vmem()], [hbm()] * 4, rows, scratch_shapes=scratch)


def moment_kernel(rows_ref, x_ref, out_ref):
    x = x_ref[...]
    whitened = lax.dot_general(rows_ref[...], x, ROWS_ROWS, preferred_element_type=f32)
    out_ref[...] = jnp.dot(whitened.astype(bf16), x, preferred_element_type=f32).astype(bf16)


def moment_of(rows, x):
    return pl.pallas_call(
        moment_kernel,
        out_shape=jax.ShapeDtypeStruct(rows.shape, bf16),
        in_specs=[vmem()] * 2,
        out_specs=vmem(),
        compiler_params=pltpu.CompilerParams(vmem_limit_bytes=VMEM_LIMIT),
        cost_estimate=pl.CostEstimate(
            flops=4 * rows.size * x.shape[0], bytes_accessed=2 * x.size, transcendentals=0
        ),
        name="moment",
    )(rows, x)


def join_kernel(*refs):
    moments, far_gradients, out_ref = refs[:4], refs[4:8], refs[8]
    gradients, staged, sems, out_sems = refs[9:]
    arriving = run_copies([(ref, gradients.at[d]) for d, ref in enumerate(far_gradients)], sems)
    for f in range(8):
        total = moments[0][f].astype(f32)
        for part in moments[1:]:
            total = total + part[f].astype(f32)
        staged[f, :16] = total.astype(bf16)
    for copy in arriving:
        copy.wait()
    leaving = []
    for f in range(8):
        total = gradients[0, f].astype(f32)
        for d in range(1, 4):
            total = total + gradients[d, f].astype(f32)
        staged[f, 16:] = total.astype(bf16)
        copy = pltpu.make_async_copy(staged.at[f], out_ref.at[f], out_sems.at[f])
        copy.start()
        leaving.append(copy)
    for copy in leaving:
        copy.wait()


def join(moments, gradients):
    width = gradients[0].shape[2]
    moments = [m.reshape(8, 16, width) for m in moments]
    shape = pltpu.HBM((8, 32, width), bf16)
    scratch = [
        pltpu.VMEM((4, 8, 16, width), bf16),
        pltpu.VMEM(shape.shape, bf16),
        pltpu.SemaphoreType.DMA((4,)),
        pltpu.SemaphoreType.DMA((8,)),
    ]
    specs = [vmem()] * 4 + [hbm()] * 4
    gradients = [pltpu.with_memory_space_constraint(g, pltpu.HBM) for g in gradients]
    return call(join_kernel, shape, specs, hbm(), *moments, *gradients, scratch_shapes=scratch)


def finish_kernel(tokens, *refs):
    sums_ref, own_ref, blocks = refs[0], refs[1], refs[2:10]
    new_ref, direction_ref, rows, sems = refs[10:]
    pairs = [(block, rows.at[pl.ds(k * 128, 128)]) for k, block in enumerate(blocks)]
    copies = run_copies(pairs, sems)
    _, _, yh, zh, _ = position()
    at = (2 * yh + zh) * 16
    own = own_ref[...]
    total = sums_ref[0].astype(f32)
    for k in range(1, 8):
        total = total + sums_ref[k].astype(f32)
    inner_rows = total[:16] / tokens + damping * own.astype(bf16).astype(f32)
    high = inner_rows.astype(bf16)
    low = (inner_rows - high.astype(f32)).astype(bf16)
    left = jnp.concatenate([high, low, total[16:].astype(bf16)], axis=0)
    for copy in copies:
        copy.wait()
    product = lax.dot_general(left, rows[...], ROWS_ROWS, preferred_element_type=f32)
    curve = product[:16] + product[16:32]
    column = lax.broadcasted_iota(jnp.int32, curve.shape, 1)
    row = lax.broadcasted_iota(jnp.int32, curve.shape, 0)
    curve = curve - (column == row + at).astype(f32)
    right = jnp.concatenate([curve.astype(bf16), product[32:].astype(bf16)], axis=0)
    result = jnp.dot(right, rows[...], preferred_element_type=f32)
    new_ref[...] = own - 0.5 * step_size * result[:16]
    direction_ref[...] = result[16:]


def finish(tokens, sums, own, blocks):
    blocks = [pltpu.with_memory_space_constraint(block, pltpu.HBM) for block in blocks]
    scratch = [
        pltpu.VMEM((8 * 128, own.shape[1]), bf16),
        pltpu.SemaphoreType.DMA((8,)),
    ]
    return call(
        functools.partial(finish_kernel, tokens),
        [jax.ShapeDtypeStruct(own.shape, f32)] * 2,
        [vmem()] * 2 + [hbm()] * 8,
        [vmem()] * 2,
        sums,
        own,
        *blocks,
        scratch_shapes=scratch,
    )


def on_device(activations, cotangent, factor):
    seq_count = lax.axis_size(SEQ)
    owned = factor.shape[1]
    width = factor.shape[0]
    total_tokens = activations.shape[0] * seq_count

    def turn(block, pairs):
        return lax.ppermute(block, SEQ_GRP, pairs)

    own = factor.T
    blocks = exchange(spread(own, 16), COSETS)

    gradient_part = lax.dot_general(
        cotangent, activations, TOKENS_FIRST, preferred_element_type=f32
    ).astype(bf16)
    parts = pick(gradient_part.reshape(2 * seq_count, owned, width))
    gradients = [parts[0]]
    for d in (1, 2, 3):
        gradients.append(turn(parts[d], INNER[d]))

    blocks = blocks.reshape(2, 8 * owned, width)
    mine = own_class(blocks)
    near = [mine]
    for d in (1, 2, 3):
        near.append(turn(mine, INNER[d]))
    moments = [moment_of(mine, activations)]
    for d in (1, 2, 3):
        moment = moment_of(near[d], activations)
        moments.append(turn(moment, INNER[d]))
    other, side, corner = others(blocks)
    far = [other]
    for d, block in ((1, side), (2, mine), (3, corner)):
        far.append(turn(block, OUTER[d]))
    joined = join(moments, gradients)
    sums = exchange(joined, FAR_GROUPS)

    new_factor, direction = finish(total_tokens, sums, own, near + far)
    return (new_factor.T, direction.T)


def solution(mesh):
    torus = Mesh(
        mesh.devices.reshape(4, 8, mesh.shape["blk"], mesh.shape["grp"]),
        ("seq_0", "seq_1", "blk", "grp"),
    )
    return jax.shard_map(
        on_device,
        mesh=torus,
        in_specs=(P(SEQ, "blk"), P(SEQ, None), P("blk", SEQ_GRP)),
        out_specs=(P("blk", SEQ_GRP), P("blk", SEQ_GRP)),
        check_vma=False,
    )
```

```python
import functools

import jax
import jax.numpy as jnp
from jax import lax
from jax.experimental import pallas as pl
from jax.experimental.pallas import tpu as pltpu
from jax.sharding import Mesh
from jax.sharding import PartitionSpec as P


SEQ = ("seq_0", "seq_1")
SEQ_GRP = ("seq_0", "seq_1", "grp")
PLANES = ("seq_0", "seq_1", "blk", "grp")


damping = 0.25
step_size = 0.4

f32, bf16 = jnp.float32, jnp.bfloat16
VMEM_LIMIT = 16 * 1024 * 1024
ROWS_ROWS = (((1,), (1,)), ((), ()))
TOKENS_FIRST = (((0,), (0,)), ((), ()))

BLOCKS = 8


def device(z, y, blk):
    core = blk % 2
    z, y = (z - core) % 8, (y - core) % 8
    return ((z % 4 * 8 + y) * BLOCKS + blk) * 2 + z // 4


FAR_GROUPS = [
    [
        device(4 * (h ^ (yh & 1)) + 2 * zh + b, 2 * yh + a, blk)
        for yh in range(4)
        for zh in range(2)
    ]
    for blk in range(BLOCKS)
    for h in range(2)
    for a in range(2)
    for b in range(2)
]


def moves(step_z, step_y):
    return [
        (device(z, y, blk), device(step_z(z), step_y(y), blk))
        for z in range(8)
        for y in range(8)
        for blk in range(BLOCKS)
    ]


def stay(at):
    return at


def inner(at):
    return at ^ 1


def outer(at):
    return (at - 1) % 8 if at % 2 == 0 else (at + 1) % 8


INNER = {1: moves(inner, stay), 2: moves(stay, inner), 3: moves(inner, inner)}
ACROSS = moves(stay, outer)


def exchange(blocks, groups):
    return lax.all_to_all(
        blocks, PLANES, split_axis=0, concat_axis=0, tiled=True, axis_index_groups=groups
    )


def vmem():
    return pl.BlockSpec(memory_space=pltpu.VMEM)


def hbm():
    return pl.BlockSpec(memory_space=pltpu.HBM)


def run_copies(pairs, sems):
    copies = [pltpu.make_async_copy(*pair, sems.at[k]) for k, pair in enumerate(pairs)]
    for copy in copies:
        copy.start()
    return copies


def position():
    core = lax.axis_index("blk") & 1
    z = (lax.axis_index("grp") * 4 + lax.axis_index("seq_0") + core) & 7
    y = (lax.axis_index("seq_1") + core) & 7
    yh, zh, half = y >> 1, (z & 3) >> 1, z >> 2
    return core, y & 1, z & 1, yh, zh, half ^ (yh & 1)


def call(kernel, out_shape, in_specs, out_specs, *args, **more):
    return pl.pallas_call(
        kernel,
        out_shape=out_shape,
        in_specs=in_specs,
        out_specs=out_specs,
        compiler_params=pltpu.CompilerParams(vmem_limit_bytes=VMEM_LIMIT),
        **more,
    )(*args)


def spread_kernel(own_ref, out_ref, low, sems):
    low[...] = own_ref[...].astype(bf16)
    for copy in run_copies([(low, out_ref.at[k]) for k in range(out_ref.shape[0])], sems):
        copy.wait()


def spread(own, count):
    shape = pltpu.HBM((count,) + own.shape, bf16)
    scratch = [pltpu.VMEM(own.shape, bf16), pltpu.SemaphoreType.DMA((count,))]
    return call(spread_kernel, shape, [vmem()], hbm(), own, scratch_shapes=scratch)


def pick_kernel(rows_ref, *refs):
    out_refs, sems = refs[:4], refs[4]
    core, a, b, _, _, h = position()
    pairs = []
    for d, out_ref in enumerate(out_refs):
        for f in range(8):
            row, column = f >> 1, f & 1
            z = 4 * (h ^ (row & 1)) + 2 * column + (b ^ (d & 1))
            y = 2 * row + (a ^ (d >> 1))
            z, y = (z + 8 - core) & 7, (y + 8 - core) & 7
            there = ((z & 3) * 8 + y) * 2 + (z >> 2)
            pairs.append((rows_ref.at[there], out_ref.at[f]))
    for copy in run_copies(pairs, sems):
        copy.wait()


def pick(rows):
    shape = pltpu.HBM((8,) + rows.shape[1:], rows.dtype)
    scratch = [pltpu.SemaphoreType.DMA((32,))]
    return call(pick_kernel, [shape] * 4, [vmem()], [hbm()] * 4, rows, scratch_shapes=scratch)


def moment_kernel(rows_ref, x_ref, out_ref):
    x = x_ref[...]
    whitened = lax.dot_general(rows_ref[...], x, ROWS_ROWS, preferred_element_type=f32)
    out_ref[...] = jnp.dot(whitened.astype(bf16), x, preferred_element_type=f32).astype(bf16)


def moment_of(rows, x):
    return pl.pallas_call(
        moment_kernel,
        out_shape=jax.ShapeDtypeStruct(rows.shape, bf16),
        in_specs=[vmem()] * 2,
        out_specs=vmem(),
        compiler_params=pltpu.CompilerParams(vmem_limit_bytes=VMEM_LIMIT),
        cost_estimate=pl.CostEstimate(
            flops=4 * rows.size * x.shape[0], bytes_accessed=2 * x.size, transcendentals=0
        ),
        name="moment",
    )(rows, x)


def join_kernel(*refs):
    moments, gradients, out_ref, staged, sems = refs[:4], refs[4:8], refs[8], refs[9], refs[10]
    leaving = []
    for f in range(8):
        for first, parts in ((0, moments), (16, gradients)):
            total = parts[0][f].astype(f32)
            for part in parts[1:]:
                total = total + part[f].astype(f32)
            staged[f, first : first + 16] = total.astype(bf16)
        copy = pltpu.make_async_copy(staged.at[f], out_ref.at[f], sems.at[f])
        copy.start()
        leaving.append(copy)
    for copy in leaving:
        copy.wait()


def join(moments, gradients):
    width = gradients[0].shape[2]
    moments = [m.reshape(8, 16, width) for m in moments]
    shape = pltpu.HBM((8, 32, width), bf16)
    scratch = [pltpu.VMEM(shape.shape, bf16), pltpu.SemaphoreType.DMA((8,))]
    return call(
        join_kernel, shape, [vmem()] * 8, hbm(), *moments, *gradients, scratch_shapes=scratch
    )


def finish_kernel(tokens, *refs):
    sums_ref, own_ref, blocks = refs[0], refs[1], refs[2:4]
    new_ref, direction_ref, rows, sems = refs[4:]
    pairs = [(block, rows.at[pl.ds(k * 512, 512)]) for k, block in enumerate(blocks)]
    copies = run_copies(pairs, sems)
    _, _, _, yh, zh, _ = position()
    at = (2 * yh + zh) * 16
    own = own_ref[...]
    total = sums_ref[0].astype(f32)
    for k in range(1, 8):
        total = total + sums_ref[k].astype(f32)
    inner_rows = total[:16] / tokens + damping * own.astype(bf16).astype(f32)
    high = inner_rows.astype(bf16)
    low = (inner_rows - high.astype(f32)).astype(bf16)
    left = jnp.concatenate([high, low, total[16:].astype(bf16)], axis=0)
    for copy in copies:
        copy.wait()
    product = lax.dot_general(left, rows[...], ROWS_ROWS, preferred_element_type=f32)
    curve = product[:16] + product[16:32]
    column = lax.broadcasted_iota(jnp.int32, curve.shape, 1)
    row = lax.broadcasted_iota(jnp.int32, curve.shape, 0)
    curve = curve - (column == row + at).astype(f32)
    right = jnp.concatenate([curve.astype(bf16), product[32:].astype(bf16)], axis=0)
    result = jnp.dot(right, rows[...], preferred_element_type=f32)
    new_ref[...] = own - 0.5 * step_size * result[:16]
    direction_ref[...] = result[16:]


def finish(tokens, sums, own, blocks):
    blocks = [pltpu.with_memory_space_constraint(block, pltpu.HBM) for block in blocks]
    scratch = [
        pltpu.VMEM((2 * 512, own.shape[1]), bf16),
        pltpu.SemaphoreType.DMA((2,)),
    ]
    return call(
        functools.partial(finish_kernel, tokens),
        [jax.ShapeDtypeStruct(own.shape, f32)] * 2,
        [vmem()] * 2 + [hbm()] * 2,
        [vmem()] * 2,
        sums,
        own,
        *blocks,
        scratch_shapes=scratch,
    )


def on_device(activations, cotangent, factor):
    seq_count = lax.axis_size(SEQ)
    owned = factor.shape[1]
    width = factor.shape[0]
    total_tokens = activations.shape[0] * seq_count

    def turn(block, pairs):
        return lax.ppermute(block, PLANES, pairs)

    own = factor.T
    mine = exchange(spread(own, 8), FAR_GROUPS).reshape(8 * owned, width)

    gradient_part = lax.dot_general(
        cotangent, activations, TOKENS_FIRST, preferred_element_type=f32
    ).astype(bf16)
    parts = pick(gradient_part.reshape(2 * seq_count, owned, width))
    gradients = [parts[0]]
    for d in (1, 2, 3):
        gradients.append(turn(parts[d], INNER[d]))

    near = [mine]
    for d in (1, 2, 3):
        near.append(turn(mine, INNER[d]))
    moments = [moment_of(mine, activations)]
    for d in (1, 2, 3):
        moment = moment_of(near[d], activations)
        moments.append(turn(moment, INNER[d]))
    near = jnp.concatenate(near, axis=0)
    far = turn(near, ACROSS)
    joined = join(moments, gradients)
    sums = exchange(joined, FAR_GROUPS)

    new_factor, direction = finish(total_tokens, sums, own, [near, far])
    return (new_factor.T, direction.T)


def solution(mesh):
    torus = Mesh(
        mesh.devices.reshape(4, 8, mesh.shape["blk"], mesh.shape["grp"]),
        ("seq_0", "seq_1", "blk", "grp"),
    )
    return jax.shard_map(
        on_device,
        mesh=torus,
        in_specs=(P(SEQ, "blk"), P(SEQ, None), P("blk", SEQ_GRP)),
        out_specs=(P("blk", SEQ_GRP), P("blk", SEQ_GRP)),
        check_vma=False,
    )
```

```python
import functools

import jax
import jax.numpy as jnp
from jax import lax
from jax.experimental import pallas as pl
from jax.experimental.pallas import tpu as pltpu
from jax.sharding import Mesh
from jax.sharding import PartitionSpec as P


SEQ = ("seq_0", "seq_1")
SEQ_GRP = ("seq_0", "seq_1", "grp")
PLANES = ("seq_0", "seq_1", "blk", "grp")


damping = 0.25
step_size = 0.4

f32, bf16 = jnp.float32, jnp.bfloat16
VMEM_LIMIT = 16 * 1024 * 1024
ROWS_ROWS = (((1,), (1,)), ((), ()))
TOKENS_FIRST = (((0,), (0,)), ((), ()))

BLOCKS = 8


def device(z, y, blk):
    core = blk % 2
    z, y = (z - core) % 8, (y - core) % 8
    return ((z % 4 * 8 + y) * BLOCKS + blk) * 2 + z // 4


FAR_GROUPS = [
    [
        device(4 * (h ^ (yh & 1)) + 2 * zh + b, 2 * yh + a, blk)
        for yh in range(4)
        for zh in range(2)
    ]
    for blk in range(BLOCKS)
    for h in range(2)
    for a in range(2)
    for b in range(2)
]


SQUARES = [
    [
        device(4 * (h ^ (yh & 1)) + 2 * zh + b, 2 * yh + a, blk)
        for a in range(2)
        for b in range(2)
    ]
    for blk in range(BLOCKS)
    for h in range(2)
    for yh in range(4)
    for zh in range(2)
]


def moves(step_z, step_y):
    return [
        (device(z, y, blk), device(step_z(z), step_y(y), blk))
        for z in range(8)
        for y in range(8)
        for blk in range(BLOCKS)
    ]


def stay(at):
    return at


def inner(at):
    return at ^ 1


def outer(at):
    return (at - 1) % 8 if at % 2 == 0 else (at + 1) % 8


INNER = {1: moves(inner, stay), 2: moves(stay, inner), 3: moves(inner, inner)}
ACROSS = moves(stay, outer)


def exchange(blocks, groups):
    return lax.all_to_all(
        blocks, PLANES, split_axis=0, concat_axis=0, tiled=True, axis_index_groups=groups
    )


def vmem():
    return pl.BlockSpec(memory_space=pltpu.VMEM)


def hbm():
    return pl.BlockSpec(memory_space=pltpu.HBM)


def run_copies(pairs, sems):
    copies = [pltpu.make_async_copy(*pair, sems.at[k]) for k, pair in enumerate(pairs)]
    for copy in copies:
        copy.start()
    return copies


def position():
    core = lax.axis_index("blk") & 1
    z = (lax.axis_index("grp") * 4 + lax.axis_index("seq_0") + core) & 7
    y = (lax.axis_index("seq_1") + core) & 7
    yh, zh, half = y >> 1, (z & 3) >> 1, z >> 2
    return core, y & 1, z & 1, yh, zh, half ^ (yh & 1)


def call(kernel, out_shape, in_specs, out_specs, *args, **more):
    return pl.pallas_call(
        kernel,
        out_shape=out_shape,
        in_specs=in_specs,
        out_specs=out_specs,
        compiler_params=pltpu.CompilerParams(vmem_limit_bytes=VMEM_LIMIT),
        **more,
    )(*args)


def spread_kernel(own_ref, out_ref, low, sems):
    low[...] = own_ref[...].astype(bf16)
    for copy in run_copies([(low, out_ref.at[k]) for k in range(out_ref.shape[0])], sems):
        copy.wait()


def spread(own, count):
    shape = pltpu.HBM((count,) + own.shape, bf16)
    scratch = [pltpu.VMEM(own.shape, bf16), pltpu.SemaphoreType.DMA((count,))]
    return call(spread_kernel, shape, [vmem()], hbm(), own, scratch_shapes=scratch)


def pick_kernel(rows_ref, *refs):
    out_refs, sems = refs[:4], refs[4]
    core, a, b, _, _, h = position()
    pairs = []
    for d, out_ref in enumerate(out_refs):
        for f in range(8):
            row, column = f >> 1, f & 1
            z = 4 * (h ^ (row & 1)) + 2 * column + (b ^ (d & 1))
            y = 2 * row + (a ^ (d >> 1))
            z, y = (z + 8 - core) & 7, (y + 8 - core) & 7
            there = ((z & 3) * 8 + y) * 2 + (z >> 2)
            pairs.append((rows_ref.at[there], out_ref.at[f]))
    for copy in run_copies(pairs, sems):
        copy.wait()


def pick(rows):
    shape = pltpu.HBM((8,) + rows.shape[1:], rows.dtype)
    scratch = [pltpu.SemaphoreType.DMA((32,))]
    return call(pick_kernel, [shape] * 4, [vmem()], [hbm()] * 4, rows, scratch_shapes=scratch)


def moment_kernel(rows_ref, x_ref, out_ref, staged, sems):
    x = x_ref[...]
    whitened = lax.dot_general(rows_ref[...], x, ROWS_ROWS, preferred_element_type=f32)
    whitened = whitened.astype(bf16)
    leaving = []
    for k in range(2):
        part = pl.ds(k * 256, 256)
        moment = jnp.dot(whitened[k * 256 : k * 256 + 256], x, preferred_element_type=f32)
        staged[part] = moment.astype(bf16)
        copy = pltpu.make_async_copy(staged.at[part], out_ref.at[part], sems.at[k])
        copy.start()
        leaving.append(copy)
    for copy in leaving:
        copy.wait()


def moment_of(rows, x):
    scratch = [pltpu.VMEM(rows.shape, bf16), pltpu.SemaphoreType.DMA((2,))]
    shape = pltpu.HBM(rows.shape, bf16)
    return call(moment_kernel, shape, [vmem()] * 2, hbm(), rows, x, scratch_shapes=scratch)


def presum_kernel(*refs):
    parts, out_ref, staged, sem = refs[:4], refs[4], refs[5], refs[6]
    for f in range(8):
        total = parts[0][f].astype(f32)
        for part in parts[1:]:
            total = total + part[f].astype(f32)
        staged[f] = total.astype(bf16)
    copy = pltpu.make_async_copy(staged, out_ref, sem)
    copy.start()
    copy.wait()


def presum(parts):
    shape = pltpu.HBM(parts[0].shape, bf16)
    scratch = [pltpu.VMEM(shape.shape, bf16), pltpu.SemaphoreType.DMA]
    return call(presum_kernel, shape, [vmem()] * 4, hbm(), *parts, scratch_shapes=scratch)


def join_kernel(moments_ref, gradient_ref, out_ref, staged, sem, sems):
    arriving = pltpu.make_async_copy(gradient_ref, staged.at[:, pl.ds(16, 16)], sem)
    arriving.start()
    for f in range(8):
        total = moments_ref[0, f].astype(f32)
        for k in range(1, 4):
            total = total + moments_ref[k, f].astype(f32)
        staged[f, :16] = total.astype(bf16)
    arriving.wait()
    leaving = run_copies([(staged.at[f], out_ref.at[f]) for f in range(8)], sems)
    for copy in leaving:
        copy.wait()


def join(moments, gradient):
    gradient = pltpu.with_memory_space_constraint(gradient, pltpu.HBM)
    shape = pltpu.HBM((8, 32, gradient.shape[2]), bf16)
    scratch = [
        pltpu.VMEM(shape.shape, bf16),
        pltpu.SemaphoreType.DMA,
        pltpu.SemaphoreType.DMA((8,)),
    ]
    specs = [vmem(), hbm()]
    return call(join_kernel, shape, specs, hbm(), moments, gradient, scratch_shapes=scratch)


def finish_kernel(tokens, *refs):
    sums_ref, own_ref, blocks = refs[0], refs[1], refs[2:4]
    new_ref, direction_ref, rows, sems = refs[4:]
    pairs = []
    for k in range(4):
        piece = blocks[k // 2].at[pl.ds(k % 2 * 256, 256)]
        pairs.append((piece, rows.at[pl.ds(k * 256, 256)]))
    copies = run_copies(pairs, sems)
    _, a, b, yh, zh, _ = position()
    at = (2 * a + b) * 128 + (2 * yh + zh) * 16
    own = own_ref[...]
    total = sums_ref[0].astype(f32)
    for k in range(1, 8):
        total = total + sums_ref[k].astype(f32)
    inner_rows = total[:16] / tokens + damping * own.astype(bf16).astype(f32)
    high = inner_rows.astype(bf16)
    low = (inner_rows - high.astype(f32)).astype(bf16)
    left = jnp.concatenate([high, low, total[16:].astype(bf16)], axis=0)
    result = jnp.zeros((32, own.shape[1]), f32)
    for k, copy in enumerate(copies):
        copy.wait()
        part = rows[pl.ds(k * 256, 256)]
        product = lax.dot_general(left, part, ROWS_ROWS, preferred_element_type=f32)
        curve = product[:16] + product[16:32]
        if k < 2:
            column = lax.broadcasted_iota(jnp.int32, curve.shape, 1) + k * 256
            row = lax.broadcasted_iota(jnp.int32, curve.shape, 0)
            curve = curve - (column == row + at).astype(f32)
        right = jnp.concatenate([curve.astype(bf16), product[32:].astype(bf16)], axis=0)
        result = result + jnp.dot(right, part, preferred_element_type=f32)
    new_ref[...] = own - 0.5 * step_size * result[:16]
    direction_ref[...] = result[16:]


def finish(tokens, sums, own, blocks):
    blocks = [pltpu.with_memory_space_constraint(block, pltpu.HBM) for block in blocks]
    scratch = [
        pltpu.VMEM((2 * 512, own.shape[1]), bf16),
        pltpu.SemaphoreType.DMA((4,)),
    ]
    return call(
        functools.partial(finish_kernel, tokens),
        [jax.ShapeDtypeStruct(own.shape, f32)] * 2,
        [vmem()] * 2 + [hbm()] * 2,
        [vmem()] * 2,
        sums,
        own,
        *blocks,
        scratch_shapes=scratch,
    )


def on_device(activations, cotangent, factor):
    seq_count = lax.axis_size(SEQ)
    owned = factor.shape[1]
    width = factor.shape[0]
    total_tokens = activations.shape[0] * seq_count

    def turn(block, pairs):
        return lax.ppermute(block, PLANES, pairs)

    own = factor.T
    mine = exchange(spread(own, 8), FAR_GROUPS).reshape(8 * owned, width)

    gradient_part = lax.dot_general(
        cotangent, activations, TOKENS_FIRST, preferred_element_type=f32
    ).astype(bf16)
    parts = pick(gradient_part.reshape(2 * seq_count, owned, width))
    gradients = [parts[0]]
    for d in (1, 2, 3):
        gradients.append(turn(parts[d], INNER[d]))

    square = jnp.broadcast_to(mine[None], (4, 8 * owned, width))
    near = exchange(square, SQUARES).reshape(32 * owned, width)
    moments = moment_of(near, activations).reshape(4, 8 * owned, width)
    moments = exchange(moments, SQUARES).reshape(4, 8, owned, width)
    far = turn(near, ACROSS)
    gradient = presum(gradients)
    joined = join(moments, gradient)
    sums = exchange(joined, FAR_GROUPS)

    new_factor, direction = finish(total_tokens, sums, own, [near, far])
    return (new_factor.T, direction.T)


def solution(mesh):
    torus = Mesh(
        mesh.devices.reshape(4, 8, mesh.shape["blk"], mesh.shape["grp"]),
        ("seq_0", "seq_1", "blk", "grp"),
    )
    return jax.shard_map(
        on_device,
        mesh=torus,
        in_specs=(P(SEQ, "blk"), P(SEQ, None), P("blk", SEQ_GRP)),
        out_specs=(P("blk", SEQ_GRP), P("blk", SEQ_GRP)),
        check_vma=False,
    )
```

```python
import functools

import jax
import jax.numpy as jnp
from jax import lax
from jax.experimental import pallas as pl
from jax.experimental.pallas import tpu as pltpu
from jax.sharding import Mesh
from jax.sharding import PartitionSpec as P


SEQ = ("seq_0", "seq_1")
SEQ_GRP = ("seq_0", "seq_1", "grp")
PLANES = ("seq_0", "seq_1", "blk", "grp")


damping = 0.25
step_size = 0.4

f32, bf16 = jnp.float32, jnp.bfloat16
VMEM_LIMIT = 16 * 1024 * 1024
ROWS_ROWS = (((1,), (1,)), ((), ()))
TOKENS_FIRST = (((0,), (0,)), ((), ()))

BLOCKS = 8


def device(z, y, blk):
    core = blk % 2
    z, y = (z - core) % 8, (y - core) % 8
    return ((z % 4 * 8 + y) * BLOCKS + blk) * 2 + z // 4


FAR_GROUPS = [
    [
        device(4 * (h ^ (yh & 1)) + 2 * zh + b, 2 * yh + a, blk)
        for yh in range(4)
        for zh in range(2)
    ]
    for blk in range(BLOCKS)
    for h in range(2)
    for a in range(2)
    for b in range(2)
]


COSETS = [
    FAR_GROUPS[8 * blk + k] + FAR_GROUPS[8 * blk + 4 + k] for blk in range(BLOCKS) for k in range(4)
]


def moves(step_z, step_y):
    return [
        (device(z, y, blk), device(step_z(z), step_y(y), blk))
        for z in range(8)
        for y in range(8)
        for blk in range(BLOCKS)
    ]


def stay(at):
    return at


def inner(at):
    return at ^ 1


INNER = {1: moves(inner, stay), 2: moves(stay, inner), 3: moves(inner, inner)}


def exchange(blocks, groups):
    return lax.all_to_all(
        blocks, PLANES, split_axis=0, concat_axis=0, tiled=True, axis_index_groups=groups
    )


def vmem():
    return pl.BlockSpec(memory_space=pltpu.VMEM)


def hbm():
    return pl.BlockSpec(memory_space=pltpu.HBM)


def run_copies(pairs, sems):
    copies = [pltpu.make_async_copy(*pair, sems.at[k]) for k, pair in enumerate(pairs)]
    for copy in copies:
        copy.start()
    return copies


def position():
    core = lax.axis_index("blk") & 1
    z = (lax.axis_index("grp") * 4 + lax.axis_index("seq_0") + core) & 7
    y = (lax.axis_index("seq_1") + core) & 7
    yh, zh, half = y >> 1, (z & 3) >> 1, z >> 2
    return core, y & 1, z & 1, yh, zh, half ^ (yh & 1)


def call(kernel, out_shape, in_specs, out_specs, *args, **more):
    return pl.pallas_call(
        kernel,
        out_shape=out_shape,
        in_specs=in_specs,
        out_specs=out_specs,
        compiler_params=pltpu.CompilerParams(vmem_limit_bytes=VMEM_LIMIT),
        **more,
    )(*args)


def spread_kernel(own_ref, out_ref, low, sems):
    low[...] = own_ref[...].astype(bf16)
    for copy in run_copies([(low, out_ref.at[k]) for k in range(out_ref.shape[0])], sems):
        copy.wait()


def spread(own, count):
    shape = pltpu.HBM((count,) + own.shape, bf16)
    scratch = [pltpu.VMEM(own.shape, bf16), pltpu.SemaphoreType.DMA((count,))]
    return call(spread_kernel, shape, [vmem()], hbm(), own, scratch_shapes=scratch)


def pick_kernel(rows_ref, *refs):
    out_refs, sems = refs[:4], refs[4]
    core, a, b, _, _, h = position()
    pairs = []
    for d, out_ref in enumerate(out_refs):
        for f in range(8):
            row, column = f >> 1, f & 1
            z = 4 * (h ^ (row & 1)) + 2 * column + (b ^ (d & 1))
            y = 2 * row + (a ^ (d >> 1))
            z, y = (z + 8 - core) & 7, (y + 8 - core) & 7
            there = ((z & 3) * 8 + y) * 2 + (z >> 2)
            pairs.append((rows_ref.at[there], out_ref.at[f]))
    for copy in run_copies(pairs, sems):
        copy.wait()


def pick(rows):
    shape = pltpu.HBM((8,) + rows.shape[1:], rows.dtype)
    scratch = [pltpu.SemaphoreType.DMA((32,))]
    return call(pick_kernel, [shape] * 4, [vmem()], [hbm()] * 4, rows, scratch_shapes=scratch)


def moment_kernel(rows_ref, x_ref, out_ref):
    x = x_ref[...]
    rows = rows_ref[position()[5]]
    whitened = lax.dot_general(rows, x, ROWS_ROWS, preferred_element_type=f32)
    out_ref[...] = jnp.dot(whitened.astype(bf16), x, preferred_element_type=f32).astype(bf16)


def moment_of(rows, x):
    shape = jax.ShapeDtypeStruct(rows.shape[1:], bf16)
    return call(moment_kernel, shape, [vmem()] * 2, vmem(), rows, x)


def join_kernel(*refs):
    moments, gradients, out_ref = refs[:4], refs[4:8], refs[8]
    for f in range(8):
        for first, parts in ((0, moments), (16, gradients)):
            total = parts[0][f].astype(f32)
            for part in parts[1:]:
                total = total + part[f].astype(f32)
            out_ref[f, first : first + 16] = total.astype(bf16)


def join(moments, gradients):
    width = gradients[0].shape[2]
    moments = [m.reshape(8, 16, width) for m in moments]
    shape = jax.ShapeDtypeStruct((8, 32, width), bf16)
    return call(join_kernel, shape, [vmem()] * 8, vmem(), *moments, *gradients)


def finish_kernel(tokens, *refs):
    sums_ref, own_ref, blocks = refs[0], refs[1], refs[2:6]
    new_ref, direction_ref = refs[6:]
    _, _, _, yh, zh, h = position()
    at = h * 128 + (2 * yh + zh) * 16
    own = own_ref[...]
    total = sums_ref[0].astype(f32)
    for k in range(1, 8):
        total = total + sums_ref[k].astype(f32)
    inner_rows = total[:16] / tokens + damping * own.astype(bf16).astype(f32)
    high = inner_rows.astype(bf16)
    low = (inner_rows - high.astype(f32)).astype(bf16)
    left = jnp.concatenate([high, low, total[16:].astype(bf16)], axis=0)
    result = jnp.zeros((32, own.shape[1]), f32)
    for k, block in enumerate(blocks):
        part = block[...]
        product = lax.dot_general(left, part, ROWS_ROWS, preferred_element_type=f32)
        curve = product[:16] + product[16:32]
        if k == 0:
            column = lax.broadcasted_iota(jnp.int32, curve.shape, 1)
            row = lax.broadcasted_iota(jnp.int32, curve.shape, 0)
            curve = curve - (column == row + at).astype(f32)
        right = jnp.concatenate([curve.astype(bf16), product[32:].astype(bf16)], axis=0)
        result = result + jnp.dot(right, part, preferred_element_type=f32)
    new_ref[...] = own - 0.5 * step_size * result[:16]
    direction_ref[...] = result[16:]


def finish(tokens, sums, own, blocks):
    return call(
        functools.partial(finish_kernel, tokens),
        [jax.ShapeDtypeStruct(own.shape, f32)] * 2,
        [vmem()] * 6,
        [vmem()] * 2,
        sums,
        own,
        *[block.reshape(256, own.shape[1]) for block in blocks],
    )


def on_device(activations, cotangent, factor):
    seq_count = lax.axis_size(SEQ)
    owned = factor.shape[1]
    width = factor.shape[0]
    total_tokens = activations.shape[0] * seq_count

    def turn(block, pairs):
        return lax.ppermute(block, PLANES, pairs)

    own = factor.T
    mine = exchange(spread(own, 16), COSETS).reshape(2, 8 * owned, width)

    gradient_part = lax.dot_general(
        cotangent, activations, TOKENS_FIRST, preferred_element_type=f32
    ).astype(bf16)
    parts = pick(gradient_part.reshape(2 * seq_count, owned, width))
    gradients = [parts[0]]
    for d in (1, 2, 3):
        gradients.append(turn(parts[d], INNER[d]))

    near = [mine]
    for d in (1, 2, 3):
        near.append(turn(mine, INNER[d]))
    moments = [moment_of(mine, activations)]
    for d in (1, 2, 3):
        moment = moment_of(near[d], activations)
        moments.append(turn(moment, INNER[d]))
    joined = join(moments, gradients)
    sums = exchange(joined, FAR_GROUPS)

    new_factor, direction = finish(total_tokens, sums, own, near)
    return (new_factor.T, direction.T)


def solution(mesh):
    torus = Mesh(
        mesh.devices.reshape(4, 8, mesh.shape["blk"], mesh.shape["grp"]),
        ("seq_0", "seq_1", "blk", "grp"),
    )
    return jax.shard_map(
        on_device,
        mesh=torus,
        in_specs=(P(SEQ, "blk"), P(SEQ, None), P("blk", SEQ_GRP)),
        out_specs=(P("blk", SEQ_GRP), P("blk", SEQ_GRP)),
        check_vma=False,
    )
```

```python
import functools

import jax
import jax.numpy as jnp
from jax import lax
from jax.experimental import pallas as pl
from jax.experimental.pallas import tpu as pltpu
from jax.sharding import Mesh
from jax.sharding import PartitionSpec as P


SEQ = ("seq_0", "seq_1")
SEQ_GRP = ("seq_0", "seq_1", "grp")
PLANES = ("seq_0", "seq_1", "blk", "grp")


damping = 0.25
step_size = 0.4

f32, bf16 = jnp.float32, jnp.bfloat16
VMEM_LIMIT = 16 * 1024 * 1024
ROWS_ROWS = (((1,), (1,)), ((), ()))
TOKENS_FIRST = (((0,), (0,)), ((), ()))

BLOCKS = 8


def device(z, y, blk):
    core = blk % 2
    z, y = (z - core) % 8, (y - core) % 8
    return ((z % 4 * 8 + y) * BLOCKS + blk) * 2 + z // 4


FAR_GROUPS = [
    [device(4 * h + 2 * zh + b, 2 * yh + a, blk) for yh in range(4) for zh in range(2)]
    for blk in range(BLOCKS)
    for h in range(2)
    for a in range(2)
    for b in range(2)
]


COSETS = [
    FAR_GROUPS[8 * blk + k] + FAR_GROUPS[8 * blk + 4 + k] for blk in range(BLOCKS) for k in range(4)
]


SQUARES = [
    [device(4 * h + 2 * zh + b, 2 * yh + a, blk) for a in range(2) for b in range(2)]
    for blk in range(BLOCKS)
    for h in range(2)
    for yh in range(4)
    for zh in range(2)
]


def moves(step_z, step_y):
    return [
        (device(z, y, blk), device(step_z(z), step_y(y), blk))
        for z in range(8)
        for y in range(8)
        for blk in range(BLOCKS)
    ]


def stay(at):
    return at


def inner(at):
    return at ^ 1


INNER = {1: moves(inner, stay), 2: moves(stay, inner), 3: moves(inner, inner)}


def exchange(blocks, groups):
    return lax.all_to_all(
        blocks, PLANES, split_axis=0, concat_axis=0, tiled=True, axis_index_groups=groups
    )


def vmem():
    return pl.BlockSpec(memory_space=pltpu.VMEM)


def hbm():
    return pl.BlockSpec(memory_space=pltpu.HBM)


def run_copies(pairs, sems):
    copies = [pltpu.make_async_copy(*pair, sems.at[k]) for k, pair in enumerate(pairs)]
    for copy in copies:
        copy.start()
    return copies


def position():
    core = lax.axis_index("blk") & 1
    z = (lax.axis_index("grp") * 4 + lax.axis_index("seq_0") + core) & 7
    y = (lax.axis_index("seq_1") + core) & 7
    return core, y & 1, z & 1, y >> 1, (z & 3) >> 1, z >> 2


def call(kernel, out_shape, in_specs, out_specs, *args, **more):
    return pl.pallas_call(
        kernel,
        out_shape=out_shape,
        in_specs=in_specs,
        out_specs=out_specs,
        compiler_params=pltpu.CompilerParams(vmem_limit_bytes=VMEM_LIMIT),
        **more,
    )(*args)


def spread_kernel(own_ref, out_ref, low, sems):
    low[...] = own_ref[...].astype(bf16)
    for copy in run_copies([(low, out_ref.at[k]) for k in range(out_ref.shape[0])], sems):
        copy.wait()


def spread(own, count):
    shape = pltpu.HBM((count,) + own.shape, bf16)
    scratch = [pltpu.VMEM(own.shape, bf16), pltpu.SemaphoreType.DMA((count,))]
    return call(spread_kernel, shape, [vmem()], hbm(), own, scratch_shapes=scratch)


def pick_kernel(rows_ref, *refs):
    out_refs, sems = refs[:4], refs[4]
    core, a, b, _, _, h = position()
    pairs = []
    for d, out_ref in enumerate(out_refs):
        for f in range(8):
            row, column = f >> 1, f & 1
            z = 4 * h + 2 * column + (b ^ (d & 1))
            y = 2 * row + (a ^ (d >> 1))
            z, y = (z + 8 - core) & 7, (y + 8 - core) & 7
            there = ((z & 3) * 8 + y) * 2 + (z >> 2)
            pairs.append((rows_ref.at[there], out_ref.at[f]))
    for copy in run_copies(pairs, sems):
        copy.wait()


def pick(rows):
    shape = pltpu.HBM((8,) + rows.shape[1:], rows.dtype)
    scratch = [pltpu.SemaphoreType.DMA((32,))]
    return call(pick_kernel, [shape] * 4, [vmem()], [hbm()] * 4, rows, scratch_shapes=scratch)


def own_moment_kernel(rows_ref, far_x_ref, x_ref, out_ref, sems):
    pieces = [pl.ds(k * 256, 256) for k in range(4)]
    arriving = run_copies([(far_x_ref.at[piece], x_ref.at[piece]) for piece in pieces], sems)
    rows = rows_ref[position()[5]]
    total = jnp.zeros(out_ref.shape, f32)
    for piece, copy in zip(pieces, arriving):
        copy.wait()
        x = x_ref[piece]
        whitened = lax.dot_general(rows, x, ROWS_ROWS, preferred_element_type=f32)
        total = total + jnp.dot(whitened.astype(bf16), x, preferred_element_type=f32)
    out_ref[...] = total.astype(bf16)


def own_moment(rows, x):
    shapes = [
        jax.ShapeDtypeStruct(x.shape, bf16),
        jax.ShapeDtypeStruct(rows.shape[1:], bf16),
    ]
    x = pltpu.with_memory_space_constraint(x, pltpu.HBM)
    scratch = [pltpu.SemaphoreType.DMA((4,))]
    specs = [vmem(), hbm()]
    return call(own_moment_kernel, shapes, specs, [vmem()] * 2, rows, x, scratch_shapes=scratch)


def moments_kernel(x_ref, own_ref, *refs):
    blocks, out_ref, rows = refs[:3], refs[3], refs[4]
    _, a, b, _, _, h = position()
    me = 2 * a + b
    out_ref[me] = own_ref[...]
    for k, block in enumerate(blocks):
        rows[pl.ds(k * 128, 128)] = block[h]
    x = x_ref[...]
    whitened = lax.dot_general(rows[...], x, ROWS_ROWS, preferred_element_type=f32)
    total = jnp.dot(whitened.astype(bf16), x, preferred_element_type=f32).astype(bf16)
    for k in range(3):
        out_ref[me ^ (k + 1)] = total[k * 128 : k * 128 + 128]


def moments_of(x, own, blocks):
    shape = jax.ShapeDtypeStruct((4,) + own.shape, bf16)
    scratch = [pltpu.VMEM((3 * 128, x.shape[1]), bf16)]
    return call(
        moments_kernel, shape, [vmem()] * 5, vmem(), x, own, *blocks, scratch_shapes=scratch
    )


def join_kernel(moments_ref, *refs):
    gradients, out_ref = refs[:4], refs[4]
    for f in range(8):
        total = moments_ref[0, f].astype(f32)
        for k in range(1, 4):
            total = total + moments_ref[k, f].astype(f32)
        out_ref[f, :16] = total.astype(bf16)
        total = gradients[0][f].astype(f32)
        for part in gradients[1:]:
            total = total + part[f].astype(f32)
        out_ref[f, 16:] = total.astype(bf16)


def join(moments, gradients):
    shape = jax.ShapeDtypeStruct((8, 32, moments.shape[3]), bf16)
    return call(join_kernel, shape, [vmem()] * 5, vmem(), moments, *gradients)


def finish_kernel(tokens, *refs):
    sums_ref, own_ref, blocks = refs[0], refs[1], refs[2:6]
    new_ref, direction_ref = refs[6:]
    _, _, _, yh, zh, h = position()
    at = h * 128 + (2 * yh + zh) * 16
    own = own_ref[...]
    total = sums_ref[0].astype(f32)
    for k in range(1, 8):
        total = total + sums_ref[k].astype(f32)
    inner_rows = total[:16] / tokens + damping * own.astype(bf16).astype(f32)
    high = inner_rows.astype(bf16)
    low = (inner_rows - high.astype(f32)).astype(bf16)
    left = jnp.concatenate([high, low, total[16:].astype(bf16)], axis=0)
    result = jnp.zeros((32, own.shape[1]), f32)
    for k, block in enumerate(blocks):
        part = block[...]
        product = lax.dot_general(left, part, ROWS_ROWS, preferred_element_type=f32)
        curve = product[:16] + product[16:32]
        if k == 0:
            column = lax.broadcasted_iota(jnp.int32, curve.shape, 1)
            row = lax.broadcasted_iota(jnp.int32, curve.shape, 0)
            curve = curve - (column == row + at).astype(f32)
        right = jnp.concatenate([curve.astype(bf16), product[32:].astype(bf16)], axis=0)
        result = result + jnp.dot(right, part, preferred_element_type=f32)
    new_ref[...] = own - 0.5 * step_size * result[:16]
    direction_ref[...] = result[16:]


def finish(tokens, sums, own, blocks):
    return call(
        functools.partial(finish_kernel, tokens),
        [jax.ShapeDtypeStruct(own.shape, f32)] * 2,
        [vmem()] * 6,
        [vmem()] * 2,
        sums,
        own,
        *[block.reshape(256, own.shape[1]) for block in blocks],
    )


def on_device(activations, cotangent, factor):
    seq_count = lax.axis_size(SEQ)
    owned = factor.shape[1]
    width = factor.shape[0]
    total_tokens = activations.shape[0] * seq_count

    def turn(block, pairs):
        return lax.ppermute(block, PLANES, pairs)

    own = factor.T
    mine = exchange(spread(own, 16), COSETS).reshape(2, 8 * owned, width)

    gradient_part = lax.dot_general(
        cotangent, activations, TOKENS_FIRST, preferred_element_type=f32
    ).astype(bf16)
    parts = pick(gradient_part.reshape(2 * seq_count, owned, width))
    gradients = [parts[0]]
    for d in (1, 2, 3):
        gradients.append(turn(parts[d], INNER[d]))

    near = [mine]
    for d in (1, 2, 3):
        near.append(turn(mine, INNER[d]))
    x, moment = own_moment(mine, activations)
    moments = moments_of(x, moment, near[1:])
    moments, *gradients = lax.optimization_barrier((moments, *gradients))
    moments = exchange(moments, SQUARES).reshape(4, 8, owned, width)
    joined = join(moments, gradients)
    sums = exchange(joined, FAR_GROUPS)

    new_factor, direction = finish(total_tokens, sums, own, near)
    return (new_factor.T, direction.T)


def solution(mesh):
    torus = Mesh(
        mesh.devices.reshape(4, 8, mesh.shape["blk"], mesh.shape["grp"]),
        ("seq_0", "seq_1", "blk", "grp"),
    )
    return jax.shard_map(
        on_device,
        mesh=torus,
        in_specs=(P(SEQ, "blk"), P(SEQ, None), P("blk", SEQ_GRP)),
        out_specs=(P("blk", SEQ_GRP), P("blk", SEQ_GRP)),
        check_vma=False,
    )
```

```python
import functools

import jax
import jax.numpy as jnp
from jax import lax
from jax.experimental import pallas as pl
from jax.experimental.pallas import tpu as pltpu
from jax.sharding import Mesh
from jax.sharding import PartitionSpec as P


SEQ = ("seq_0", "seq_1")
SEQ_GRP = ("seq_0", "seq_1", "grp")
PLANES = ("seq_0", "seq_1", "blk", "grp")


damping = 0.25
step_size = 0.4

f32, bf16 = jnp.float32, jnp.bfloat16
VMEM_LIMIT = 16 * 1024 * 1024
ROWS_ROWS = (((1,), (1,)), ((), ()))
TOKENS_FIRST = (((0,), (0,)), ((), ()))

BLOCKS = 8


def device(z, y, blk):
    core = blk % 2
    z, y = (z - core) % 8, (y - core) % 8
    return ((z % 4 * 8 + y) * BLOCKS + blk) * 2 + z // 4


FAR_GROUPS = [
    [device(4 * h + 2 * zh + b, 2 * yh + a, blk) for yh in range(4) for zh in range(2)]
    for blk in range(BLOCKS)
    for h in range(2)
    for a in range(2)
    for b in range(2)
]


COSETS = [
    FAR_GROUPS[8 * blk + k] + FAR_GROUPS[8 * blk + 4 + k] for blk in range(BLOCKS) for k in range(4)
]


def moves(step_z, step_y):
    return [
        (device(z, y, blk), device(step_z(z), step_y(y), blk))
        for z in range(8)
        for y in range(8)
        for blk in range(BLOCKS)
    ]


def stay(at):
    return at


def inner(at):
    return at ^ 1


INNER = {1: moves(inner, stay), 2: moves(stay, inner), 3: moves(inner, inner)}


def exchange(blocks, groups):
    return lax.all_to_all(
        blocks, PLANES, split_axis=0, concat_axis=0, tiled=True, axis_index_groups=groups
    )


def vmem():
    return pl.BlockSpec(memory_space=pltpu.VMEM)


def hbm():
    return pl.BlockSpec(memory_space=pltpu.HBM)


def run_copies(pairs, sems):
    copies = [pltpu.make_async_copy(*pair, sems.at[k]) for k, pair in enumerate(pairs)]
    for copy in copies:
        copy.start()
    return copies


def position():
    core = lax.axis_index("blk") & 1
    z = (lax.axis_index("grp") * 4 + lax.axis_index("seq_0") + core) & 7
    y = (lax.axis_index("seq_1") + core) & 7
    return core, y & 1, z & 1, y >> 1, (z & 3) >> 1, z >> 2


def call(kernel, out_shape, in_specs, out_specs, *args, **more):
    return pl.pallas_call(
        kernel,
        out_shape=out_shape,
        in_specs=in_specs,
        out_specs=out_specs,
        compiler_params=pltpu.CompilerParams(vmem_limit_bytes=VMEM_LIMIT),
        **more,
    )(*args)


def spread_kernel(far_own_ref, out_ref, own, low, sem, sems):
    arriving = pltpu.make_async_copy(far_own_ref, own, sem)
    arriving.start()
    arriving.wait()
    low[...] = own[...].astype(bf16)
    for copy in run_copies([(low, out_ref.at[k]) for k in range(out_ref.shape[0])], sems):
        copy.wait()


def spread(own, count):
    own = pltpu.with_memory_space_constraint(own, pltpu.HBM)
    shape = pltpu.HBM((count,) + own.shape, bf16)
    scratch = [
        pltpu.VMEM(own.shape, f32),
        pltpu.VMEM(own.shape, bf16),
        pltpu.SemaphoreType.DMA,
        pltpu.SemaphoreType.DMA((count,)),
    ]
    return call(spread_kernel, shape, [hbm()], hbm(), own, scratch_shapes=scratch)


def pick_kernel(rows_ref, *refs):
    out_refs, sems = refs[:4], refs[4]
    core, a, b, _, _, h = position()
    pairs = []
    for d, out_ref in enumerate(out_refs):
        for f in range(8):
            row, column = f >> 1, f & 1
            z = 4 * h + 2 * column + (b ^ (d & 1))
            y = 2 * row + (a ^ (d >> 1))
            z, y = (z + 8 - core) & 7, (y + 8 - core) & 7
            there = ((z & 3) * 8 + y) * 2 + (z >> 2)
            pairs.append((rows_ref.at[there], out_ref.at[f]))
    for copy in run_copies(pairs, sems):
        copy.wait()


def pick(rows):
    shape = pltpu.HBM((8,) + rows.shape[1:], rows.dtype)
    scratch = [pltpu.SemaphoreType.DMA((32,))]
    return call(pick_kernel, [shape] * 4, [vmem()], [hbm()] * 4, rows, scratch_shapes=scratch)


def moment_kernel(rows_ref, x_ref, out_ref):
    x = x_ref[...]
    rows = rows_ref[position()[5]]
    whitened = lax.dot_general(rows, x, ROWS_ROWS, preferred_element_type=f32)
    out_ref[...] = jnp.dot(whitened.astype(bf16), x, preferred_element_type=f32).astype(bf16)


def moment_of(rows, x):
    shape = jax.ShapeDtypeStruct(rows.shape[1:], bf16)
    return call(moment_kernel, shape, [vmem()] * 2, vmem(), rows, x)


def join_kernel(*refs):
    moments, gradients, out_ref = refs[:4], refs[4:8], refs[8]
    for f in range(8):
        for first, parts in ((0, moments), (16, gradients)):
            total = parts[0][f].astype(f32)
            for part in parts[1:]:
                total = total + part[f].astype(f32)
            out_ref[f, first : first + 16] = total.astype(bf16)


def join(moments, gradients):
    width = gradients[0].shape[2]
    moments = [m.reshape(8, 16, width) for m in moments]
    shape = jax.ShapeDtypeStruct((8, 32, width), bf16)
    return call(join_kernel, shape, [vmem()] * 8, vmem(), *moments, *gradients)


def finish_kernel(tokens, *refs):
    sums_ref, own_ref, blocks = refs[0], refs[1], refs[2:6]
    new_ref, direction_ref = refs[6:]
    _, _, _, yh, zh, h = position()
    at = h * 128 + (2 * yh + zh) * 16
    own = own_ref[...]
    total = sums_ref[0].astype(f32)
    for k in range(1, 8):
        total = total + sums_ref[k].astype(f32)
    inner_rows = total[:16] / tokens + damping * own.astype(bf16).astype(f32)
    high = inner_rows.astype(bf16)
    low = (inner_rows - high.astype(f32)).astype(bf16)
    left = jnp.concatenate([high, low, total[16:].astype(bf16)], axis=0)
    result = jnp.zeros((32, own.shape[1]), f32)
    for k, block in enumerate(blocks):
        part = block[...]
        product = lax.dot_general(left, part, ROWS_ROWS, preferred_element_type=f32)
        curve = product[:16] + product[16:32]
        if k == 0:
            column = lax.broadcasted_iota(jnp.int32, curve.shape, 1)
            row = lax.broadcasted_iota(jnp.int32, curve.shape, 0)
            curve = curve - (column == row + at).astype(f32)
        right = jnp.concatenate([curve.astype(bf16), product[32:].astype(bf16)], axis=0)
        result = result + jnp.dot(right, part, preferred_element_type=f32)
    new_ref[...] = own - 0.5 * step_size * result[:16]
    direction_ref[...] = result[16:]


def finish(tokens, sums, own, blocks):
    return call(
        functools.partial(finish_kernel, tokens),
        [jax.ShapeDtypeStruct(own.shape, f32)] * 2,
        [vmem()] * 6,
        [vmem()] * 2,
        sums,
        own,
        *[block.reshape(256, own.shape[1]) for block in blocks],
    )


def on_device(activations, cotangent, factor):
    seq_count = lax.axis_size(SEQ)
    owned = factor.shape[1]
    width = factor.shape[0]
    total_tokens = activations.shape[0] * seq_count

    def turn(block, pairs):
        return lax.ppermute(block, PLANES, pairs)

    own = factor.T
    mine = exchange(spread(own, 16), COSETS).reshape(2, 8 * owned, width)

    gradient_part = lax.dot_general(
        cotangent, activations, TOKENS_FIRST, preferred_element_type=f32
    ).astype(bf16)
    parts = pick(gradient_part.reshape(2 * seq_count, owned, width))
    gradients = [parts[0]]
    for d in (1, 2, 3):
        gradients.append(turn(parts[d], INNER[d]))

    near = [mine]
    for d in (1, 2, 3):
        near.append(turn(mine, INNER[d]))
    moments = [moment_of(mine, activations)]
    for d in (1, 2, 3):
        moment = moment_of(near[d], activations)
        moments.append(turn(moment, INNER[d]))
    joined = join(moments, gradients)
    sums = exchange(joined, FAR_GROUPS)

    new_factor, direction = finish(total_tokens, sums, own, near)
    return (new_factor.T, direction.T)


def solution(mesh):
    torus = Mesh(
        mesh.devices.reshape(4, 8, mesh.shape["blk"], mesh.shape["grp"]),
        ("seq_0", "seq_1", "blk", "grp"),
    )
    return jax.shard_map(
        on_device,
        mesh=torus,
        in_specs=(P(SEQ, "blk"), P(SEQ, None), P("blk", SEQ_GRP)),
        out_specs=(P("blk", SEQ_GRP), P("blk", SEQ_GRP)),
        check_vma=False,
    )
```

```python
import functools

import jax
import jax.numpy as jnp
from jax import lax
from jax.experimental import pallas as pl
from jax.experimental.pallas import tpu as pltpu
from jax.sharding import Mesh
from jax.sharding import PartitionSpec as P


SEQ = ("seq_0", "seq_1")
SEQ_GRP = ("seq_0", "seq_1", "grp")
PLANES = ("seq_0", "seq_1", "blk", "grp")


damping = 0.25
step_size = 0.4

f32, bf16 = jnp.float32, jnp.bfloat16
VMEM_LIMIT = 16 * 1024 * 1024
ROWS_ROWS = (((1,), (1,)), ((), ()))
TOKENS_FIRST = (((0,), (0,)), ((), ()))

BLOCKS = 8


def device(z, y, blk):
    core = blk % 2
    z, y = (z - core) % 8, (y - core) % 8
    return ((z % 4 * 8 + y) * BLOCKS + blk) * 2 + z // 4


FAR_GROUPS = [
    [device(4 * h + 2 * zh + b, 2 * yh + a, blk) for yh in range(4) for zh in range(2)]
    for blk in range(BLOCKS)
    for h in range(2)
    for a in range(2)
    for b in range(2)
]


COSETS = [
    FAR_GROUPS[8 * blk + k] + FAR_GROUPS[8 * blk + 4 + k] for blk in range(BLOCKS) for k in range(4)
]


def moves(step_z, step_y):
    return [
        (device(z, y, blk), device(step_z(z), step_y(y), blk))
        for z in range(8)
        for y in range(8)
        for blk in range(BLOCKS)
    ]


def stay(at):
    return at


def inner(at):
    return at ^ 1


INNER = {1: moves(inner, stay), 2: moves(stay, inner), 3: moves(inner, inner)}
ORDER = (3, 1, 2)


def exchange(blocks, groups):
    return lax.all_to_all(
        blocks, PLANES, split_axis=0, concat_axis=0, tiled=True, axis_index_groups=groups
    )


def vmem():
    return pl.BlockSpec(memory_space=pltpu.VMEM)


def hbm():
    return pl.BlockSpec(memory_space=pltpu.HBM)


def run_copies(pairs, sems):
    copies = [pltpu.make_async_copy(*pair, sems.at[k]) for k, pair in enumerate(pairs)]
    for copy in copies:
        copy.start()
    return copies


def position():
    core = lax.axis_index("blk") & 1
    z = (lax.axis_index("grp") * 4 + lax.axis_index("seq_0") + core) & 7
    y = (lax.axis_index("seq_1") + core) & 7
    return core, y & 1, z & 1, y >> 1, (z & 3) >> 1, z >> 2


def call(kernel, out_shape, in_specs, out_specs, *args, **more):
    return pl.pallas_call(
        kernel,
        out_shape=out_shape,
        in_specs=in_specs,
        out_specs=out_specs,
        compiler_params=pltpu.CompilerParams(vmem_limit_bytes=VMEM_LIMIT),
        **more,
    )(*args)


def spread_kernel(far_own_ref, out_ref, own, low, sem, sems):
    arriving = pltpu.make_async_copy(far_own_ref, own, sem)
    arriving.start()
    arriving.wait()
    low[...] = own[...].astype(bf16)
    for copy in run_copies([(low, out_ref.at[k]) for k in range(out_ref.shape[0])], sems):
        copy.wait()


def spread(own, count):
    own = pltpu.with_memory_space_constraint(own, pltpu.HBM)
    shape = pltpu.HBM((count,) + own.shape, bf16)
    scratch = [
        pltpu.VMEM(own.shape, f32),
        pltpu.VMEM(own.shape, bf16),
        pltpu.SemaphoreType.DMA,
        pltpu.SemaphoreType.DMA((count,)),
    ]
    return call(spread_kernel, shape, [hbm()], hbm(), own, scratch_shapes=scratch)


def pick_kernel(rows_ref, *refs):
    out_refs, sems = refs[:4], refs[4]
    core, a, b, _, _, h = position()
    pairs = []
    for d, out_ref in enumerate(out_refs):
        for f in range(8):
            row, column = f >> 1, f & 1
            z = 4 * h + 2 * column + (b ^ (d & 1))
            y = 2 * row + (a ^ (d >> 1))
            z, y = (z + 8 - core) & 7, (y + 8 - core) & 7
            there = ((z & 3) * 8 + y) * 2 + (z >> 2)
            pairs.append((rows_ref.at[there], out_ref.at[f]))
    for copy in run_copies(pairs, sems):
        copy.wait()


def pick(rows):
    shape = pltpu.HBM((8,) + rows.shape[1:], rows.dtype)
    scratch = [pltpu.SemaphoreType.DMA((32,))]
    return call(pick_kernel, [shape] * 4, [vmem()], [hbm()] * 4, rows, scratch_shapes=scratch)


def moment_kernel(rows_ref, x_ref, out_ref):
    x = x_ref[...]
    rows = rows_ref[position()[5]]
    whitened = lax.dot_general(rows, x, ROWS_ROWS, preferred_element_type=f32)
    out_ref[...] = jnp.dot(whitened.astype(bf16), x, preferred_element_type=f32).astype(bf16)


def moment_of(rows, x):
    shape = jax.ShapeDtypeStruct(rows.shape[1:], bf16)
    return call(moment_kernel, shape, [vmem()] * 2, vmem(), rows, x)


def join_kernel(*refs):
    moments, gradients, out_ref = refs[:4], refs[4:8], refs[8]
    for f in range(8):
        for first, parts in ((0, moments), (16, gradients)):
            total = parts[0][f].astype(f32)
            for part in parts[1:]:
                total = total + part[f].astype(f32)
            out_ref[f, first : first + 16] = total.astype(bf16)


def join(moments, gradients):
    width = gradients[0].shape[2]
    moments = [m.reshape(8, 16, width) for m in moments]
    shape = jax.ShapeDtypeStruct((8, 32, width), bf16)
    return call(join_kernel, shape, [vmem()] * 8, vmem(), *moments, *gradients)


def finish_kernel(tokens, *refs):
    sums_ref, own_ref, blocks = refs[0], refs[1], refs[2:6]
    new_ref, direction_ref = refs[6:]
    _, _, _, yh, zh, h = position()
    at = h * 128 + (2 * yh + zh) * 16
    own = own_ref[...]
    total = sums_ref[0].astype(f32)
    for k in range(1, 8):
        total = total + sums_ref[k].astype(f32)
    inner_rows = total[:16] / tokens + damping * own.astype(bf16).astype(f32)
    high = inner_rows.astype(bf16)
    low = (inner_rows - high.astype(f32)).astype(bf16)
    left = jnp.concatenate([high, low, total[16:].astype(bf16)], axis=0)
    result = jnp.zeros((32, own.shape[1]), f32)
    for k, block in enumerate(blocks):
        part = block[...]
        product = lax.dot_general(left, part, ROWS_ROWS, preferred_element_type=f32)
        curve = product[:16] + product[16:32]
        if k == 0:
            column = lax.broadcasted_iota(jnp.int32, curve.shape, 1)
            row = lax.broadcasted_iota(jnp.int32, curve.shape, 0)
            curve = curve - (column == row + at).astype(f32)
        right = jnp.concatenate([curve.astype(bf16), product[32:].astype(bf16)], axis=0)
        result = result + jnp.dot(right, part, preferred_element_type=f32)
    new_ref[...] = own - 0.5 * step_size * result[:16]
    direction_ref[...] = result[16:]


def finish(tokens, sums, own, blocks):
    return call(
        functools.partial(finish_kernel, tokens),
        [jax.ShapeDtypeStruct(own.shape, f32)] * 2,
        [vmem()] * 6,
        [vmem()] * 2,
        sums,
        own,
        *[block.reshape(256, own.shape[1]) for block in blocks],
    )


def on_device(activations, cotangent, factor):
    seq_count = lax.axis_size(SEQ)
    owned = factor.shape[1]
    width = factor.shape[0]
    total_tokens = activations.shape[0] * seq_count

    def turn(block, pairs):
        return lax.ppermute(block, PLANES, pairs)

    own = factor.T
    mine = exchange(spread(own, 16), COSETS).reshape(2, 8 * owned, width)

    gradient_part = lax.dot_general(
        cotangent, activations, TOKENS_FIRST, preferred_element_type=f32
    ).astype(bf16)
    parts = pick(gradient_part.reshape(2 * seq_count, owned, width))
    gradients = [parts[0]]
    for d in (1, 2, 3):
        gradients.append(turn(parts[d], INNER[d]))

    near = {0: mine}
    for d in ORDER:
        near[d] = turn(mine, INNER[d])
    moments = [moment_of(mine, activations)]
    for d in ORDER:
        moment = moment_of(near[d], activations)
        moments.append(turn(moment, INNER[d]))
    joined = join(moments, gradients)
    sums = exchange(joined, FAR_GROUPS)

    new_factor, direction = finish(total_tokens, sums, own, [near[d] for d in range(4)])
    return (new_factor.T, direction.T)


def solution(mesh):
    torus = Mesh(
        mesh.devices.reshape(4, 8, mesh.shape["blk"], mesh.shape["grp"]),
        ("seq_0", "seq_1", "blk", "grp"),
    )
    return jax.shard_map(
        on_device,
        mesh=torus,
        in_specs=(P(SEQ, "blk"), P(SEQ, None), P("blk", SEQ_GRP)),
        out_specs=(P("blk", SEQ_GRP), P("blk", SEQ_GRP)),
        check_vma=False,
    )
```

```python
import functools

import jax
import jax.numpy as jnp
from jax import lax
from jax.experimental import pallas as pl
from jax.experimental.pallas import tpu as pltpu
from jax.sharding import Mesh
from jax.sharding import PartitionSpec as P


SEQ = ("seq_0", "seq_1")
SEQ_GRP = ("seq_0", "seq_1", "grp")
PLANES = ("seq_0", "seq_1", "blk", "grp")


damping = 0.25
step_size = 0.4

f32, bf16 = jnp.float32, jnp.bfloat16
VMEM_LIMIT = 16 * 1024 * 1024
ROWS_ROWS = (((1,), (1,)), ((), ()))
TOKENS_FIRST = (((0,), (0,)), ((), ()))

BLOCKS = 8


def device(z, y, blk):
    core = blk % 2
    z, y = (z - core) % 8, (y - core) % 8
    return ((z % 4 * 8 + y) * BLOCKS + blk) * 2 + z // 4


FAR_GROUPS = [
    [device(4 * h + 2 * zh + b, 2 * yh + a, blk) for yh in range(4) for zh in range(2)]
    for blk in range(BLOCKS)
    for h in range(2)
    for a in range(2)
    for b in range(2)
]


COSETS = [
    FAR_GROUPS[8 * blk + k] + FAR_GROUPS[8 * blk + 4 + k] for blk in range(BLOCKS) for k in range(4)
]


def moves(step_z, step_y):
    return [
        (device(z, y, blk), device(step_z(z), step_y(y), blk))
        for z in range(8)
        for y in range(8)
        for blk in range(BLOCKS)
    ]


def stay(at):
    return at


def inner(at):
    return at ^ 1


INNER = {1: moves(inner, stay), 2: moves(stay, inner), 3: moves(inner, inner)}
ORDER = (3, 1, 2)


def exchange(blocks, groups):
    return lax.all_to_all(
        blocks, PLANES, split_axis=0, concat_axis=0, tiled=True, axis_index_groups=groups
    )


def vmem():
    return pl.BlockSpec(memory_space=pltpu.VMEM)


def hbm():
    return pl.BlockSpec(memory_space=pltpu.HBM)


def run_copies(pairs, sems):
    copies = [pltpu.make_async_copy(*pair, sems.at[k]) for k, pair in enumerate(pairs)]
    for copy in copies:
        copy.start()
    return copies


def position():
    core = lax.axis_index("blk") & 1
    z = (lax.axis_index("grp") * 4 + lax.axis_index("seq_0") + core) & 7
    y = (lax.axis_index("seq_1") + core) & 7
    return core, y & 1, z & 1, y >> 1, (z & 3) >> 1, z >> 2


def call(kernel, out_shape, in_specs, out_specs, *args, **more):
    return pl.pallas_call(
        kernel,
        out_shape=out_shape,
        in_specs=in_specs,
        out_specs=out_specs,
        compiler_params=pltpu.CompilerParams(vmem_limit_bytes=VMEM_LIMIT),
        **more,
    )(*args)


def spread_kernel(far_own_ref, out_ref, own, low, sem, sems):
    arriving = pltpu.make_async_copy(far_own_ref, own, sem)
    arriving.start()
    arriving.wait()
    low[...] = own[...].astype(bf16)
    for copy in run_copies([(low, out_ref.at[k]) for k in range(out_ref.shape[0])], sems):
        copy.wait()


def spread(own, count):
    own = pltpu.with_memory_space_constraint(own, pltpu.HBM)
    shape = pltpu.HBM((count,) + own.shape, bf16)
    scratch = [
        pltpu.VMEM(own.shape, f32),
        pltpu.VMEM(own.shape, bf16),
        pltpu.SemaphoreType.DMA,
        pltpu.SemaphoreType.DMA((count,)),
    ]
    return call(spread_kernel, shape, [hbm()], hbm(), own, scratch_shapes=scratch)


def pick_kernel(rows_ref, *refs):
    out_refs, sems = refs[:4], refs[4]
    core, a, b, _, _, h = position()
    pairs = []
    for d, out_ref in enumerate(out_refs):
        for f in range(8):
            row, column = f >> 1, f & 1
            z = 4 * h + 2 * column + (b ^ (d & 1))
            y = 2 * row + (a ^ (d >> 1))
            z, y = (z + 8 - core) & 7, (y + 8 - core) & 7
            there = ((z & 3) * 8 + y) * 2 + (z >> 2)
            pairs.append((rows_ref.at[there], out_ref.at[f]))
    for copy in run_copies(pairs, sems):
        copy.wait()


def pick(rows):
    shape = pltpu.HBM((8,) + rows.shape[1:], rows.dtype)
    scratch = [pltpu.SemaphoreType.DMA((32,))]
    return call(pick_kernel, [shape] * 4, [vmem()], [hbm()] * 4, rows, scratch_shapes=scratch)


def gram_part(rows, x):
    whitened = lax.dot_general(rows, x, ROWS_ROWS, preferred_element_type=f32)
    return jnp.dot(whitened.astype(bf16), x, preferred_element_type=f32).astype(bf16)


def own_rows_kernel(rows_ref, x_ref, out_ref):
    out_ref[...] = rows_ref[position()[5]]


def own_rows(rows, x):
    shape = jax.ShapeDtypeStruct(rows.shape[1:], bf16)
    return call(own_rows_kernel, shape, [vmem()] * 2, vmem(), rows, x)


def own_moment_kernel(rows_ref, x_ref, out_ref):
    out_ref[...] = gram_part(rows_ref[...], x_ref[...])


def own_moment(rows, x):
    shape = jax.ShapeDtypeStruct(rows.shape, bf16)
    return call(own_moment_kernel, shape, [vmem()] * 2, vmem(), rows, x)


def moment_kernel(rows_ref, x_ref, out_ref):
    out_ref[...] = gram_part(rows_ref[position()[5]], x_ref[...])


def moment_of(rows, x):
    shape = jax.ShapeDtypeStruct(rows.shape[1:], bf16)
    return call(moment_kernel, shape, [vmem()] * 2, vmem(), rows, x)


def join_kernel(*refs):
    moments, gradients, out_ref = refs[:4], refs[4:8], refs[8]
    for f in range(8):
        for first, parts in ((0, moments), (16, gradients)):
            total = parts[0][f].astype(f32)
            for part in parts[1:]:
                total = total + part[f].astype(f32)
            out_ref[f, first : first + 16] = total.astype(bf16)


def join(moments, gradients):
    width = gradients[0].shape[2]
    moments = [m.reshape(8, 16, width) for m in moments]
    shape = jax.ShapeDtypeStruct((8, 32, width), bf16)
    return call(join_kernel, shape, [vmem()] * 8, vmem(), *moments, *gradients)


def finish_kernel(tokens, *refs):
    sums_ref, own_ref, blocks = refs[0], refs[1], refs[2:6]
    new_ref, direction_ref, rows = refs[6:]
    _, _, _, yh, zh, h = position()
    at = h * 128 + (2 * yh + zh) * 16
    own = own_ref[...]
    total = sums_ref[0].astype(f32)
    for k in range(1, 8):
        total = total + sums_ref[k].astype(f32)
    inner_rows = total[:16] / tokens + damping * own.astype(bf16).astype(f32)
    high = inner_rows.astype(bf16)
    low = (inner_rows - high.astype(f32)).astype(bf16)
    left = jnp.concatenate([high, low, total[16:].astype(bf16)], axis=0)
    for k, block in enumerate(blocks):
        rows[pl.ds(k * 256, 256)] = block[...]
    product = lax.dot_general(left, rows[...], ROWS_ROWS, preferred_element_type=f32)
    curve = product[:16] + product[16:32]
    column = lax.broadcasted_iota(jnp.int32, curve.shape, 1)
    row = lax.broadcasted_iota(jnp.int32, curve.shape, 0)
    curve = curve - (column == row + at).astype(f32)
    right = jnp.concatenate([curve.astype(bf16), product[32:].astype(bf16)], axis=0)
    result = jnp.dot(right, rows[...], preferred_element_type=f32)
    new_ref[...] = own - 0.5 * step_size * result[:16]
    direction_ref[...] = result[16:]


def finish(tokens, sums, own, blocks):
    return call(
        functools.partial(finish_kernel, tokens),
        [jax.ShapeDtypeStruct(own.shape, f32)] * 2,
        [vmem()] * 6,
        [vmem()] * 2,
        sums,
        own,
        *[block.reshape(256, own.shape[1]) for block in blocks],
        scratch_shapes=[pltpu.VMEM((4 * 256, own.shape[1]), bf16)],
    )


def on_device(activations, cotangent, factor):
    seq_count = lax.axis_size(SEQ)
    owned = factor.shape[1]
    width = factor.shape[0]
    total_tokens = activations.shape[0] * seq_count

    def turn(block, pairs):
        return lax.ppermute(block, PLANES, pairs)

    own = factor.T
    mine = exchange(spread(own, 16), COSETS).reshape(2, 8 * owned, width)

    gradient_part = lax.dot_general(
        cotangent, activations, TOKENS_FIRST, preferred_element_type=f32
    ).astype(bf16)
    parts = pick(gradient_part.reshape(2 * seq_count, owned, width))
    gradients = [parts[0]]
    for d in (1, 2, 3):
        gradients.append(turn(parts[d], INNER[d]))

    near = {0: mine}
    for d in ORDER:
        near[d] = turn(mine, INNER[d])
    own_block = own_rows(mine, activations)
    moments = [own_moment(own_block, activations)]
    for d in ORDER:
        moment = moment_of(near[d], activations)
        moments.append(turn(moment, INNER[d]))
    joined = join(moments, gradients)
    sums = exchange(joined, FAR_GROUPS)

    new_factor, direction = finish(total_tokens, sums, own, [near[d] for d in range(4)])
    return (new_factor.T, direction.T)


def solution(mesh):
    torus = Mesh(
        mesh.devices.reshape(4, 8, mesh.shape["blk"], mesh.shape["grp"]),
        ("seq_0", "seq_1", "blk", "grp"),
    )
    return jax.shard_map(
        on_device,
        mesh=torus,
        in_specs=(P(SEQ, "blk"), P(SEQ, None), P("blk", SEQ_GRP)),
        out_specs=(P("blk", SEQ_GRP), P("blk", SEQ_GRP)),
        check_vma=False,
    )
```

```python
import functools

import jax
import jax.numpy as jnp
from jax import lax
from jax.experimental import pallas as pl
from jax.experimental.pallas import tpu as pltpu
from jax.sharding import Mesh
from jax.sharding import PartitionSpec as P


SEQ = ("seq_0", "seq_1")
SEQ_GRP = ("seq_0", "seq_1", "grp")
PLANES = ("seq_0", "seq_1", "blk", "grp")


damping = 0.25
step_size = 0.4

f32, bf16 = jnp.float32, jnp.bfloat16
VMEM_LIMIT = 16 * 1024 * 1024
ROWS_ROWS = (((1,), (1,)), ((), ()))
TOKENS_FIRST = (((0,), (0,)), ((), ()))

BLOCKS = 8


def device(z, y, blk):
    core = blk % 2
    z, y = (z - core) % 8, (y - core) % 8
    return ((z % 4 * 8 + y) * BLOCKS + blk) * 2 + z // 4


FAR_GROUPS = [
    [device(4 * h + 2 * zh + b, 2 * yh + a, blk) for yh in range(4) for zh in range(2)]
    for blk in range(BLOCKS)
    for h in range(2)
    for a in range(2)
    for b in range(2)
]


COSETS = [
    FAR_GROUPS[8 * blk + k] + FAR_GROUPS[8 * blk + 4 + k] for blk in range(BLOCKS) for k in range(4)
]


def moves(step_z, step_y):
    return [
        (device(z, y, blk), device(step_z(z), step_y(y), blk))
        for z in range(8)
        for y in range(8)
        for blk in range(BLOCKS)
    ]


def stay(at):
    return at


def inner(at):
    return at ^ 1


INNER = {1: moves(inner, stay), 2: moves(stay, inner), 3: moves(inner, inner)}
ORDER = (3, 2, 1)


def exchange(blocks, groups):
    return lax.all_to_all(
        blocks, PLANES, split_axis=0, concat_axis=0, tiled=True, axis_index_groups=groups
    )


def vmem():
    return pl.BlockSpec(memory_space=pltpu.VMEM)


def hbm():
    return pl.BlockSpec(memory_space=pltpu.HBM)


def run_copies(pairs, sems):
    copies = [pltpu.make_async_copy(*pair, sems.at[k]) for k, pair in enumerate(pairs)]
    for copy in copies:
        copy.start()
    return copies


def position():
    core = lax.axis_index("blk") & 1
    z = (lax.axis_index("grp") * 4 + lax.axis_index("seq_0") + core) & 7
    y = (lax.axis_index("seq_1") + core) & 7
    return core, y & 1, z & 1, y >> 1, (z & 3) >> 1, z >> 2


def call(kernel, out_shape, in_specs, out_specs, *args, **more):
    return pl.pallas_call(
        kernel,
        out_shape=out_shape,
        in_specs=in_specs,
        out_specs=out_specs,
        compiler_params=pltpu.CompilerParams(vmem_limit_bytes=VMEM_LIMIT),
        **more,
    )(*args)


def spread_kernel(far_own_ref, out_ref, own, low, sem, sems):
    arriving = pltpu.make_async_copy(far_own_ref, own, sem)
    arriving.start()
    arriving.wait()
    low[...] = own[...].astype(bf16)
    for copy in run_copies([(low, out_ref.at[k]) for k in range(out_ref.shape[0])], sems):
        copy.wait()


def spread(own, count):
    own = pltpu.with_memory_space_constraint(own, pltpu.HBM)
    shape = pltpu.HBM((count,) + own.shape, bf16)
    scratch = [
        pltpu.VMEM(own.shape, f32),
        pltpu.VMEM(own.shape, bf16),
        pltpu.SemaphoreType.DMA,
        pltpu.SemaphoreType.DMA((count,)),
    ]
    return call(spread_kernel, shape, [hbm()], hbm(), own, scratch_shapes=scratch)


def pick_kernel(rows_ref, *refs):
    out_refs, sems = refs[:4], refs[4]
    core, a, b, _, _, h = position()
    pairs = []
    for d, out_ref in enumerate(out_refs):
        for f in range(8):
            row, column = f >> 1, f & 1
            z = 4 * h + 2 * column + (b ^ (d & 1))
            y = 2 * row + (a ^ (d >> 1))
            z, y = (z + 8 - core) & 7, (y + 8 - core) & 7
            there = ((z & 3) * 8 + y) * 2 + (z >> 2)
            pairs.append((rows_ref.at[there], out_ref.at[f]))
    for copy in run_copies(pairs, sems):
        copy.wait()


def pick(rows):
    shape = pltpu.HBM((8,) + rows.shape[1:], rows.dtype)
    scratch = [pltpu.SemaphoreType.DMA((32,))]
    return call(pick_kernel, [shape] * 4, [vmem()], [hbm()] * 4, rows, scratch_shapes=scratch)


def gram_part(rows, x):
    whitened = lax.dot_general(rows, x, ROWS_ROWS, preferred_element_type=f32)
    return jnp.dot(whitened.astype(bf16), x, preferred_element_type=f32).astype(bf16)


def own_rows_kernel(rows_ref, out_ref):
    out_ref[...] = rows_ref[position()[5]]


def own_rows(rows):
    shape = jax.ShapeDtypeStruct(rows.shape[1:], bf16)
    return call(own_rows_kernel, shape, [vmem()], vmem(), rows)


def other_rows_kernel(rows_ref, x_ref, out_ref):
    out_ref[...] = rows_ref[1 - position()[5]]


def other_rows(rows, x):
    shape = jax.ShapeDtypeStruct(rows.shape[1:], bf16)
    return call(other_rows_kernel, shape, [vmem()] * 2, vmem(), rows, x)


def own_moment_kernel(rows_ref, x_ref, out_ref):
    out_ref[...] = gram_part(rows_ref[...], x_ref[...])


def own_moment(rows, x):
    shape = jax.ShapeDtypeStruct(rows.shape, bf16)
    return call(own_moment_kernel, shape, [vmem()] * 2, vmem(), rows, x)


def moment_kernel(rows_ref, x_ref, out_ref):
    out_ref[...] = gram_part(rows_ref[position()[5]], x_ref[...])


def moment_of(rows, x):
    shape = jax.ShapeDtypeStruct(rows.shape[1:], bf16)
    return call(moment_kernel, shape, [vmem()] * 2, vmem(), rows, x)


def join_kernel(*refs):
    moments, gradients, out_ref = refs[:4], refs[4:8], refs[8]
    for f in range(8):
        for first, parts in ((0, moments), (16, gradients)):
            total = parts[0][f].astype(f32)
            for part in parts[1:]:
                total = total + part[f].astype(f32)
            out_ref[f, first : first + 16] = total.astype(bf16)


def join(moments, gradients):
    width = gradients[0].shape[2]
    moments = [m.reshape(8, 16, width) for m in moments]
    shape = jax.ShapeDtypeStruct((8, 32, width), bf16)
    return call(join_kernel, shape, [vmem()] * 8, vmem(), *moments, *gradients)


def panel_kernel(tokens, sums_ref, own_ref, out_ref):
    total = sums_ref[0].astype(f32)
    for k in range(1, 8):
        total = total + sums_ref[k].astype(f32)
    inner_rows = total[:16] / tokens + damping * own_ref[...].astype(bf16).astype(f32)
    high = inner_rows.astype(bf16)
    low = (inner_rows - high.astype(f32)).astype(bf16)
    out_ref[...] = jnp.concatenate([high, low, total[16:].astype(bf16)], axis=0)


def panel(tokens, sums, own):
    shape = jax.ShapeDtypeStruct((48, own.shape[1]), bf16)
    kernel = functools.partial(panel_kernel, tokens)
    return call(kernel, shape, [vmem()] * 2, vmem(), sums, own)


def finish_kernel(left_ref, own_ref, *refs):
    blocks, new_ref, direction_ref, rows = refs[:-3], refs[-3], refs[-2], refs[-1]
    _, _, _, yh, zh, h = position()
    at = h * 128 + (2 * yh + zh) * 16
    own = own_ref[...]
    first = 0
    for block in blocks:
        rows[pl.ds(first, block.shape[0])] = block[...]
        first += block.shape[0]
    product = lax.dot_general(left_ref[...], rows[...], ROWS_ROWS, preferred_element_type=f32)
    curve = product[:16] + product[16:32]
    column = lax.broadcasted_iota(jnp.int32, curve.shape, 1)
    row = lax.broadcasted_iota(jnp.int32, curve.shape, 0)
    curve = curve - (column == row + at).astype(f32)
    right = jnp.concatenate([curve.astype(bf16), product[32:].astype(bf16)], axis=0)
    result = jnp.dot(right, rows[...], preferred_element_type=f32)
    new_ref[...] = own - 0.5 * step_size * result[:16]
    direction_ref[...] = result[16:]


def finish(left, own, blocks):
    width = own.shape[1]
    return call(
        finish_kernel,
        [jax.ShapeDtypeStruct(own.shape, f32)] * 2,
        [vmem()] * (2 + len(blocks)),
        [vmem()] * 2,
        left,
        own,
        *[block.reshape(-1, width) for block in blocks],
        scratch_shapes=[pltpu.VMEM((width, width), bf16)],
    )


def on_device(activations, cotangent, factor):
    seq_count = lax.axis_size(SEQ)
    owned = factor.shape[1]
    width = factor.shape[0]
    total_tokens = activations.shape[0] * seq_count

    def turn(block, pairs):
        return lax.ppermute(block, PLANES, pairs)

    own = factor.T
    mine = exchange(spread(own, 16), COSETS).reshape(2, 8 * owned, width)

    gradient_part = lax.dot_general(
        cotangent, activations, TOKENS_FIRST, preferred_element_type=f32
    ).astype(bf16)
    parts = pick(gradient_part.reshape(2 * seq_count, owned, width))
    gradients = [parts[0]]
    for d in (1, 2, 3):
        gradients.append(turn(parts[d], INNER[d]))

    own_block = own_rows(mine)
    near = {}
    for d in ORDER:
        near[d] = turn(own_block if d == 3 else mine, INNER[d])
    other_block = other_rows(mine, activations)
    moments = [own_moment(own_block, activations)]
    for d in ORDER:
        moment = (own_moment if d == 3 else moment_of)(near[d], activations)
        moments.append(turn(moment, INNER[d]))
    late = turn(other_block, INNER[3])
    joined = join(moments, gradients)
    sums = exchange(joined, FAR_GROUPS)

    left = panel(total_tokens, sums, own)
    new_factor, direction = finish(left, own, [mine, near[1], near[2], near[3], late])
    return (new_factor.T, direction.T)


def solution(mesh):
    torus = Mesh(
        mesh.devices.reshape(4, 8, mesh.shape["blk"], mesh.shape["grp"]),
        ("seq_0", "seq_1", "blk", "grp"),
    )
    return jax.shard_map(
        on_device,
        mesh=torus,
        in_specs=(P(SEQ, "blk"), P(SEQ, None), P("blk", SEQ_GRP)),
        out_specs=(P("blk", SEQ_GRP), P("blk", SEQ_GRP)),
        check_vma=False,
    )
```

```python
import functools

import jax
import jax.numpy as jnp
from jax import lax
from jax.experimental import pallas as pl
from jax.experimental.pallas import tpu as pltpu
from jax.sharding import Mesh
from jax.sharding import PartitionSpec as P


SEQ = ("seq_0", "seq_1")
SEQ_GRP = ("seq_0", "seq_1", "grp")
PLANES = ("seq_0", "seq_1", "blk", "grp")


damping = 0.25
step_size = 0.4

f32, bf16 = jnp.float32, jnp.bfloat16
VMEM_LIMIT = 16 * 1024 * 1024
ROWS_ROWS = (((1,), (1,)), ((), ()))
TOKENS_FIRST = (((0,), (0,)), ((), ()))

BLOCKS = 8


def device(z, y, blk):
    core = blk % 2
    z, y = (z - core) % 8, (y - core) % 8
    return ((z % 4 * 8 + y) * BLOCKS + blk) * 2 + z // 4


FAR_GROUPS = [
    [device(4 * h + 2 * zh + b, 2 * yh + a, blk) for yh in range(4) for zh in range(2)]
    for blk in range(BLOCKS)
    for h in range(2)
    for a in range(2)
    for b in range(2)
]


COSETS = [
    FAR_GROUPS[8 * blk + k] + FAR_GROUPS[8 * blk + 4 + k] for blk in range(BLOCKS) for k in range(4)
]


def moves(step_z, step_y):
    return [
        (device(z, y, blk), device(step_z(z), step_y(y), blk))
        for z in range(8)
        for y in range(8)
        for blk in range(BLOCKS)
    ]


def stay(at):
    return at


def inner(at):
    return at ^ 1


INNER = {1: moves(inner, stay), 2: moves(stay, inner), 3: moves(inner, inner)}
ORDER = (3, 2, 1)


def exchange(blocks, groups):
    return lax.all_to_all(
        blocks, PLANES, split_axis=0, concat_axis=0, tiled=True, axis_index_groups=groups
    )


def vmem():
    return pl.BlockSpec(memory_space=pltpu.VMEM)


def hbm():
    return pl.BlockSpec(memory_space=pltpu.HBM)


def run_copies(pairs, sems):
    copies = [pltpu.make_async_copy(*pair, sems.at[k]) for k, pair in enumerate(pairs)]
    for copy in copies:
        copy.start()
    return copies


def position():
    core = lax.axis_index("blk") & 1
    z = (lax.axis_index("grp") * 4 + lax.axis_index("seq_0") + core) & 7
    y = (lax.axis_index("seq_1") + core) & 7
    return core, y & 1, z & 1, y >> 1, (z & 3) >> 1, z >> 2


def call(kernel, out_shape, in_specs, out_specs, *args, **more):
    return pl.pallas_call(
        kernel,
        out_shape=out_shape,
        in_specs=in_specs,
        out_specs=out_specs,
        compiler_params=pltpu.CompilerParams(vmem_limit_bytes=VMEM_LIMIT),
        **more,
    )(*args)


def spread_kernel(far_own_ref, out_ref, own, low, sem, sems):
    arriving = pltpu.make_async_copy(far_own_ref, own, sem)
    arriving.start()
    arriving.wait()
    low[...] = own[...].astype(bf16)
    for copy in run_copies([(low, out_ref.at[k]) for k in range(out_ref.shape[0])], sems):
        copy.wait()


def spread(own, count):
    own = pltpu.with_memory_space_constraint(own, pltpu.HBM)
    shape = pltpu.HBM((count,) + own.shape, bf16)
    scratch = [
        pltpu.VMEM(own.shape, f32),
        pltpu.VMEM(own.shape, bf16),
        pltpu.SemaphoreType.DMA,
        pltpu.SemaphoreType.DMA((count,)),
    ]
    return call(spread_kernel, shape, [hbm()], hbm(), own, scratch_shapes=scratch)


def pick_kernel(rows_ref, *refs):
    out_refs, sems = refs[:4], refs[4]
    core, a, b, _, _, h = position()
    pairs = []
    for d, out_ref in enumerate(out_refs):
        for f in range(8):
            row, column = f >> 1, f & 1
            z = 4 * h + 2 * column + (b ^ (d & 1))
            y = 2 * row + (a ^ (d >> 1))
            z, y = (z + 8 - core) & 7, (y + 8 - core) & 7
            there = ((z & 3) * 8 + y) * 2 + (z >> 2)
            pairs.append((rows_ref.at[there], out_ref.at[f]))
    for copy in run_copies(pairs, sems):
        copy.wait()


def pick(rows):
    shape = pltpu.HBM((8,) + rows.shape[1:], rows.dtype)
    scratch = [pltpu.SemaphoreType.DMA((32,))]
    return call(pick_kernel, [shape] * 4, [vmem()], [hbm()] * 4, rows, scratch_shapes=scratch)


def gram_part(rows, x):
    whitened = lax.dot_general(rows, x, ROWS_ROWS, preferred_element_type=f32)
    return jnp.dot(whitened.astype(bf16), x, preferred_element_type=f32).astype(bf16)


def own_rows_kernel(rows_ref, out_ref):
    out_ref[...] = rows_ref[position()[5]]


def own_rows(rows):
    shape = jax.ShapeDtypeStruct(rows.shape[1:], bf16)
    return call(own_rows_kernel, shape, [vmem()], vmem(), rows)


def other_rows_kernel(rows_ref, x_ref, out_ref):
    out_ref[...] = rows_ref[1 - position()[5]]


def other_rows(rows, x):
    shape = jax.ShapeDtypeStruct(rows.shape[1:], bf16)
    return call(other_rows_kernel, shape, [vmem()] * 2, vmem(), rows, x)


def pair_kernel(own_ref, rows_ref, x_ref, own_out_ref, out_ref, both):
    both[:128] = own_ref[...]
    both[128:] = rows_ref[...]
    total = gram_part(both[...], x_ref[...])
    own_out_ref[...] = total[:128]
    out_ref[...] = total[128:]


def moment_pair(own, rows, x):
    shape = jax.ShapeDtypeStruct(rows.shape, bf16)
    scratch = [pltpu.VMEM((256, x.shape[1]), bf16)]
    return call(
        pair_kernel, [shape] * 2, [vmem()] * 3, [vmem()] * 2, own, rows, x, scratch_shapes=scratch
    )


def moment_kernel(rows_ref, x_ref, out_ref):
    out_ref[...] = gram_part(rows_ref[position()[5]], x_ref[...])


def moment_of(rows, x):
    shape = jax.ShapeDtypeStruct(rows.shape[1:], bf16)
    return call(moment_kernel, shape, [vmem()] * 2, vmem(), rows, x)


def join_kernel(*refs):
    moments, gradients, out_ref = refs[:4], refs[4:8], refs[8]
    for f in range(8):
        for first, parts in ((0, moments), (16, gradients)):
            total = parts[0][f].astype(f32)
            for part in parts[1:]:
                total = total + part[f].astype(f32)
            out_ref[f, first : first + 16] = total.astype(bf16)


def join(moments, gradients):
    width = gradients[0].shape[2]
    moments = [m.reshape(8, 16, width) for m in moments]
    shape = jax.ShapeDtypeStruct((8, 32, width), bf16)
    return call(join_kernel, shape, [vmem()] * 8, vmem(), *moments, *gradients)


def panel_kernel(tokens, sums_ref, own_ref, out_ref):
    total = sums_ref[0].astype(f32)
    for k in range(1, 8):
        total = total + sums_ref[k].astype(f32)
    inner_rows = total[:16] / tokens + damping * own_ref[...].astype(bf16).astype(f32)
    high = inner_rows.astype(bf16)
    low = (inner_rows - high.astype(f32)).astype(bf16)
    out_ref[...] = jnp.concatenate([high, low, total[16:].astype(bf16)], axis=0)


def panel(tokens, sums, own):
    shape = jax.ShapeDtypeStruct((48, own.shape[1]), bf16)
    kernel = functools.partial(panel_kernel, tokens)
    return call(kernel, shape, [vmem()] * 2, vmem(), sums, own)


def finish_kernel(left_ref, own_ref, *refs):
    blocks, new_ref, direction_ref, rows = refs[:-3], refs[-3], refs[-2], refs[-1]
    _, _, _, yh, zh, h = position()
    at = h * 128 + (2 * yh + zh) * 16
    own = own_ref[...]
    first = 0
    for block in blocks:
        rows[pl.ds(first, block.shape[0])] = block[...]
        first += block.shape[0]
    product = lax.dot_general(left_ref[...], rows[...], ROWS_ROWS, preferred_element_type=f32)
    curve = product[:16] + product[16:32]
    column = lax.broadcasted_iota(jnp.int32, curve.shape, 1)
    row = lax.broadcasted_iota(jnp.int32, curve.shape, 0)
    curve = curve - (column == row + at).astype(f32)
    right = jnp.concatenate([curve.astype(bf16), product[32:].astype(bf16)], axis=0)
    result = jnp.dot(right, rows[...], preferred_element_type=f32)
    new_ref[...] = own - 0.5 * step_size * result[:16]
    direction_ref[...] = result[16:]


def finish(left, own, blocks):
    width = own.shape[1]
    return call(
        finish_kernel,
        [jax.ShapeDtypeStruct(own.shape, f32)] * 2,
        [vmem()] * (2 + len(blocks)),
        [vmem()] * 2,
        left,
        own,
        *[block.reshape(-1, width) for block in blocks],
        scratch_shapes=[pltpu.VMEM((width, width), bf16)],
    )


def on_device(activations, cotangent, factor):
    seq_count = lax.axis_size(SEQ)
    owned = factor.shape[1]
    width = factor.shape[0]
    total_tokens = activations.shape[0] * seq_count

    def turn(block, pairs):
        return lax.ppermute(block, PLANES, pairs)

    own = factor.T
    mine = exchange(spread(own, 16), COSETS).reshape(2, 8 * owned, width)

    gradient_part = lax.dot_general(
        cotangent, activations, TOKENS_FIRST, preferred_element_type=f32
    ).astype(bf16)
    parts = pick(gradient_part.reshape(2 * seq_count, owned, width))
    gradients = [parts[0]]
    for d in (1, 2, 3):
        gradients.append(turn(parts[d], INNER[d]))

    own_block = own_rows(mine)
    near = {}
    for d in ORDER:
        near[d] = turn(own_block if d == 3 else mine, INNER[d])
    other_block = other_rows(mine, activations)
    moments = []
    for d in ORDER:
        if d == 3:
            own_part, moment = moment_pair(own_block, near[d], activations)
            moments.append(own_part)
        else:
            moment = moment_of(near[d], activations)
        moments.append(turn(moment, INNER[d]))
    late = turn(other_block, INNER[3])
    joined = join(moments, gradients)
    sums = exchange(joined, FAR_GROUPS)

    left = panel(total_tokens, sums, own)
    new_factor, direction = finish(left, own, [mine, near[1], near[2], near[3], late])
    return (new_factor.T, direction.T)


def solution(mesh):
    torus = Mesh(
        mesh.devices.reshape(4, 8, mesh.shape["blk"], mesh.shape["grp"]),
        ("seq_0", "seq_1", "blk", "grp"),
    )
    return jax.shard_map(
        on_device,
        mesh=torus,
        in_specs=(P(SEQ, "blk"), P(SEQ, None), P("blk", SEQ_GRP)),
        out_specs=(P("blk", SEQ_GRP), P("blk", SEQ_GRP)),
        check_vma=False,
    )
```
